512 devices in a mesh: tile: 128 (over y, z, core), mem: 4 (over x).
Axes of the slice: x: 4, y: 8, z: 8, core: 2. Of those that a mesh axis runs over, the one named last changes fastest.
Arguments:
- field: bfloat16 [61, 2048, 1024], P(None, 'tile'), may hold values from -6 to 6
- vert_filter: bfloat16 [1, 60, 60], replicated, may hold values from -1 to 1.5
- loc_filter: bfloat16 [1, 60, 60], replicated, may hold values from -1 to 1.5
- alpha_table: float32 [16], replicated, may hold values from 0 to 1
- xscale_idx: int32 [2, 1024], replicated, may hold values from 0 to 15
- yscale_idx: int32 [2, 2048], replicated, may hold values from 0 to 15
- members: bfloat16 [4, 61, 2048, 1024], P('mem', None, 'tile'), may hold values from -6 to 6
Outputs:
- product: bfloat16 [61, 2048, 1024], P(None, ('tile', 'mem'))
The draws below stay inside these ranges and needn't reach their ends.
All inputs are finite; a program needn't handle non-finite values.
Results may differ from the reference program's by a relative error of at most 0.0075.
Values may be sent and summed in bfloat16 or wider, within the bound.
A program may use at most 128 MiB of HBM per device.

```python
import jax
import jax.numpy as jnp
from jax import lax

ROWS = 1024
VARS3 = 1
VARS2 = 1
LEV = 60
NSCALE = 16
COLS = 2048
SLABS = 61
MEMBERS = 4


def banded(key):
    first, second = jax.random.split(key)
    rows = jnp.arange(LEV)[:, None]
    cols = jnp.arange(LEV)[None, :]
    shape = (VARS3, LEV, LEV)
    off_diag = jnp.clip(0.3 * jax.random.normal(first, shape, jnp.float32), -1.0, 1.0)
    diag = 1.0 + 0.5 * jax.random.uniform(second, shape, jnp.float32)
    inside = jnp.abs(rows - cols) <= 3
    result = jnp.where(rows == cols, diag, jnp.where(inside, off_diag, 0.0))
    return result.astype(jnp.bfloat16)


def draw_vert_filter(key, part):
    return banded(jax.random.fold_in(key, 11))


def draw_loc_filter(key, part):
    return banded(jax.random.fold_in(key, 23))


def draw_alpha_table(key, part):
    first, second = jax.random.split(jax.random.fold_in(key, 37))
    order = jax.random.permutation(first, NSCALE)
    slow_count = NSCALE // 2
    slow = order < slow_count
    frac = jax.random.uniform(second, (NSCALE,), jnp.float32)
    slow_low = jnp.log(jnp.float32(COLS) * 0.5)
    slow_len = jnp.exp(slow_low + frac * jnp.log(jnp.float32(6.0)))
    fast_len = jnp.exp(jnp.log(jnp.float32(3.0)) + frac * jnp.log(jnp.float32(20.0 / 3.0)))
    scale_len = jnp.where(slow, slow_len, fast_len)
    return (1.0 - 1.0 / scale_len).astype(jnp.float32)


def set_ends(values, own_key, smallest, largest):
    shape = values.shape
    index_at = [jax.random.randint(jax.random.fold_in(own_key, axis), (), 0, shape[axis]) for axis in range(len(shape))]
    values = values.at[tuple(index_at)].set(smallest)
    longest = shape.index(max(shape))
    index_at[longest] = (index_at[longest] + 1) % shape[longest]
    return values.at[tuple(index_at)].set(largest)


def level_of(rng, extent, pieces, smallest, top_value):
    gain, own = 1.0, jax.random.fold_in(rng, 6)
    for position, blocks in pieces:
        draws = jnp.exp(jax.random.uniform(jax.random.fold_in(own, position), (blocks,), jnp.float32, smallest / len(pieces), top_value / len(pieces)))
        gain = gain * jnp.repeat(draws, extent[position] // blocks).reshape([-1 if axis == position else 1 for axis in range(len(extent))])
    return gain


def scatter_about(rng, extent, deviation, limit, pieces=(), held_as=jnp.bfloat16):
    loudness = level_of(rng, extent, pieces, -0.22, 0.18) if pieces else 1.0
    array = jax.random.normal(rng, extent, jnp.float32) * deviation * loudness
    return jnp.minimum(jnp.maximum(array, -limit), limit).astype(held_as)


def setup_inputs(seed: int = 0) -> dict:
    key_list = jax.random.split(jax.random.key(seed), 8)
    field = scatter_about(key_list[0], (SLABS, COLS, ROWS), 1.0, 6.0, ((1, 128),))
    vert_filter = draw_vert_filter(jax.random.fold_in(key_list[7], 71), 0)
    loc_filter = draw_loc_filter(jax.random.fold_in(key_list[7], 71), 0)
    alpha_table = draw_alpha_table(jax.random.fold_in(key_list[7], 71), 0)
    xscale_idx = set_ends(jax.random.randint(key_list[4], (VARS3 + VARS2, ROWS), 0, NSCALE), jax.random.fold_in(key_list[4], 1), 0, NSCALE - 1).astype(jnp.int32)
    yscale_idx = set_ends(jax.random.randint(key_list[5], (VARS3 + VARS2, COLS), 0, NSCALE), jax.random.fold_in(key_list[5], 1), 0, NSCALE - 1).astype(jnp.int32)
    members = scatter_about(key_list[6], (MEMBERS, SLABS, COLS, ROWS), 1.0, 6.0, ((0, 4), (2, 128)))
    return dict(field=field, vert_filter=vert_filter, loc_filter=loc_filter, alpha_table=alpha_table, xscale_idx=xscale_idx, yscale_idx=yscale_idx, members=members)


def slab_vars():
    three_d = jnp.repeat(jnp.arange(VARS3, dtype=jnp.int32), LEV)
    two_d = VARS3 + jnp.arange(VARS2, dtype=jnp.int32)
    return jnp.concatenate([three_d, two_d])

def vertical(matrices, values):
    level_rows = VARS3 * LEV
    stacked = values[:level_rows].astype(jnp.float32).reshape(VARS3, LEV, COLS * ROWS)
    mixed = jnp.einsum('vij,vjp->vip', matrices.astype(jnp.float32), stacked)
    mixed = mixed.reshape(level_rows, COLS, ROWS)
    return jnp.concatenate([mixed, values[level_rows:].astype(jnp.float32)], 0)

def recursive(values, alpha, axis):
    moved = jnp.moveaxis(values, axis, 0)
    gain_fwd = jnp.sqrt(1.0 - alpha * alpha)
    gain_back = (1.0 - alpha * alpha) / jnp.sqrt(1.0 + alpha * alpha)

    def forward_step(carry, column):
        carry = alpha * carry + gain_fwd * column
        return (carry, carry)
    start = jnp.zeros(moved.shape[1:], jnp.float32)
    _, forward = lax.scan(forward_step, start, moved)

    def backward_step(carry, column):
        carry = alpha * carry + gain_back * column
        return (carry, carry)
    _, backward = lax.scan(backward_step, start, forward, reverse=True)
    return jnp.moveaxis(backward, 0, axis)

def reference(field, vert_filter, loc_filter, alpha_table, xscale_idx, yscale_idx, members):
    filtered = vertical(vert_filter, field).astype(jnp.bfloat16)
    var_index = slab_vars()
    alpha_x = alpha_table[xscale_idx[var_index]]
    alpha_y = alpha_table[yscale_idx[var_index]]
    smooth_x = recursive(filtered.astype(jnp.float32), alpha_x, 1)
    static_term = recursive(smooth_x, alpha_y, 2)

    def member_step(running, member):
        scaled = (member.astype(jnp.float32) * field.astype(jnp.float32)).astype(jnp.bfloat16)
        localized = vertical(loc_filter, scaled)
        return (running + member.astype(jnp.float32) * localized, None)
    start = jnp.zeros((SLABS, COLS, ROWS), jnp.float32)
    total, _ = lax.scan(member_step, start, members)
    ens_term = total / (MEMBERS - 1)
    return (static_term + ens_term).astype(jnp.bfloat16)
```

```python
import functools

import jax
import jax.numpy as jnp
from jax import lax
from jax.experimental import pallas as pl
from jax.experimental.pallas import tpu as pltpu
from jax.sharding import PartitionSpec as P

MESH = pl.DeviceIdType.MESH
F32 = jnp.float32
BF16 = jnp.bfloat16
LANES = 128
SPAN = 16


def gains(a):
    return jnp.sqrt(1.0 - a * a), (1.0 - a * a) / jnp.sqrt(1.0 + a * a)


def extended(dst, matrix, pad):
    n = matrix.shape[-1]
    dst[...] = jnp.zeros(dst.shape, F32)
    dst[0:n, 0:n] = matrix[0].astype(F32)
    i = lax.broadcasted_iota(jnp.int32, dst.shape, 0)
    j = lax.broadcasted_iota(jnp.int32, dst.shape, 1)
    keep = (i == j) & (i >= n) & (i < pad)
    dst[...] = jnp.where(keep, 1.0, dst[...])


def kernel(
    tiles, mems, slabs,
    field, members, vert, loc, xidx, alpha, yidx,
    out,
    fbuf, mbuf, x32, m32, send_m, recv_m, own_f, ax, gfx, gbx,
    send_z, recv_z, send_c, recv_c, send_y, recv_y, pre, suf, carry,
    smooth, acc, tab, lmat, vmat,
    local_sem, sm_s, sm_r, sz_s, sz_r, sc_s, sc_r, sy_s, sy_r,
):
    tile = lax.axis_index("tile")
    mem = lax.axis_index("mem")
    groups = tiles // SPAN
    q = lax.rem(tile, SPAN)
    y = tile // SPAN
    cols = field.shape[1]
    rows = field.shape[2]
    blocks = rows // LANES
    own = cols // mems
    levels = vert.shape[-1]
    padded = x32.shape[1] // cols

    get_members = pltpu.make_async_copy(members.at[0], mbuf, local_sem.at[0])
    get_members.start()
    get_field = pltpu.make_async_copy(field, fbuf, local_sem.at[1])
    get_field.start()

    barrier = pltpu.get_barrier_semaphore()

    @pl.loop(1, mems)
    def _(d):
        pl.semaphore_signal(
            barrier, inc=1, device_id={"mem": lax.rem(mem + d, mems)}, device_id_type=MESH
        )

    @pl.loop(1, SPAN)
    def _(d):
        pl.semaphore_signal(
            barrier,
            inc=1,
            device_id={"tile": y * SPAN + lax.rem(q + d, SPAN)},
            device_id_type=MESH,
        )

    @pl.loop(1, groups)
    def _(d):
        pl.semaphore_signal(
            barrier,
            inc=1,
            device_id={"tile": lax.rem(y + d, groups) * SPAN + q},
            device_id_type=MESH,
        )

    sub = lax.broadcasted_iota(jnp.int32, (padded, LANES), 0)

    @pl.loop(0, blocks)
    def _(b):
        lane = pl.ds(pl.multiple_of(b * LANES, LANES), LANES)
        idx = xidx[:, lane]
        a = jnp.zeros(idx.shape, F32)
        for k in range(alpha.shape[0]):
            a = jnp.where(idx == k, alpha[k], a)
        wide = jnp.where(
            sub < levels,
            jnp.broadcast_to(a[0:1], (padded, LANES)),
            jnp.broadcast_to(a[1:2], (padded, LANES)),
        )
        fwd, back = gains(wide)
        ax[b] = wide
        gfx[b] = fwd
        gbx[b] = back

    extended(lmat, loc, slabs)
    extended(vmat, vert, slabs)

    def spread(src, dst):
        for b in range(blocks):
            dst[b, pl.ds(slabs * cols, (padded - slabs) * cols), :] = jnp.zeros(
                ((padded - slabs) * cols, LANES), F32
            )

        @pl.loop(0, slabs)
        def _(s):
            at = pl.ds(pl.multiple_of(s * cols, cols), cols)
            for b in range(blocks):
                dst[b, at, :] = src[s, :, b * LANES : (b + 1) * LANES].astype(F32)

    def send_member(d):
        return pltpu.make_async_remote_copy(
            src_ref=send_m.at[lax.rem(mem + d, mems)],
            dst_ref=recv_m.at[d],
            send_sem=sm_s.at[d],
            recv_sem=sm_r.at[d],
            device_id={"mem": lax.rem(mem + d, mems)},
            device_id_type=MESH,
        )

    def collect(src, dst, first):
        @pl.loop(0, own)
        def _(c):
            for b in range(blocks):
                part = src[b, pl.ds(first + c, padded, stride=cols), :]
                dst[c, :, b * LANES : (b + 1) * LANES] = part.astype(BF16)

    get_members.wait()
    spread(mbuf, m32)
    collect(m32, send_m.at[lax.rem(mem + 2, mems)], lax.rem(mem + 2, mems) * own)
    pl.semaphore_wait(barrier, (mems - 1) + (SPAN - 1) + (groups - 1))
    send_member(2).start()
    for d in (1, 3):
        peer = lax.rem(mem + d, mems)
        collect(m32, send_m.at[peer], peer * own)
        send_member(d).start()

    get_field.wait()
    spread(fbuf, x32)

    quads = padded // 16
    half = padded // 2
    per_half = half // 16

    def local_states(b, p, f, start):
        at = pl.ds(pl.multiple_of(p * 16, 16), 16)
        a, fwd, back = ax[b, at, :], gfx[b, at, :], gbx[b, at, :]
        states = []
        for c in range(cols):
            f = a * f + fwd * x32[b, pl.ds(p * 16 * cols + c, 16, stride=cols), :]
            states.append(f)
        value = start
        backs = [None] * cols
        for c in reversed(range(cols)):
            value = a * value + back * states[c]
            backs[c] = value
        return states, backs

    @pl.loop(0, blocks)
    def _(b):
        @pl.loop(0, quads)
        def _(p):
            zero = jnp.zeros((16, LANES), F32)
            states, backs = local_states(b, p, zero, zero)
            piece = 2 * b + p // per_half
            at = pl.ds(pl.multiple_of(lax.rem(p, per_half) * 16, 16), 16)
            send_z[piece, 0, at, :] = states[-1].astype(BF16)
            send_z[piece, 1, at, :] = backs[0].astype(BF16)

    def to_span(src, dst, s_sem, r_sem, d):
        peer = lax.rem(q + d, SPAN)
        return pltpu.make_async_remote_copy(
            src_ref=src.at[peer],
            dst_ref=dst.at[q],
            send_sem=s_sem.at[peer],
            recv_sem=r_sem.at[q],
            device_id={"tile": y * SPAN + peer},
            device_id_type=MESH,
        )

    def from_span(src, dst, s_sem, r_sem, d):
        peer = lax.rem(q + d, SPAN)
        return pltpu.make_async_remote_copy(
            src_ref=src.at[peer],
            dst_ref=dst.at[peer],
            send_sem=s_sem.at[peer],
            recv_sem=r_sem.at[peer],
            device_id={"tile": y * SPAN + peer},
            device_id_type=MESH,
        )

    @pl.loop(1, SPAN)
    def _(d):
        to_span(send_z, recv_z, sz_s, sz_r, d).start()

    recv_z[q] = send_z[q]

    collect(m32, send_m.at[mem], mem * own)
    collect(x32, own_f, mem * own)

    wide_lanes = 2 * LANES
    local_m = lmat[...].astype(BF16)

    def ensemble(src, first):
        @pl.loop(0, own)
        def _(c):
            for w in range(rows // wide_lanes):
                lane = slice(w * wide_lanes, (w + 1) * wide_lanes)
                m = src[c, :, lane].astype(F32)
                scaled = (m * own_f[c, :, lane].astype(F32)).astype(BF16)
                term = m * jnp.dot(local_m, scaled, preferred_element_type=F32)
                acc[c, :, lane] = term if first else acc[c, :, lane] + term

    ensemble(send_m.at[mem], True)

    lane_id = lax.broadcasted_iota(jnp.int32, (8, LANES), 1)
    sub8 = lax.broadcasted_iota(jnp.int32, (8, LANES), 0)

    @pl.loop(0, own)
    def _(c):
        col = tile * cols + mem * own + c
        a0 = jnp.full((8, LANES), alpha[yidx[0, col]], F32)
        a1 = jnp.full((8, LANES), alpha[yidx[1, col]], F32)
        for kind in range(2):
            a = a0 if kind == 0 else jnp.where(sub8 < levels % 8, a0, a1)
            fwd, back = gains(a)
            right = jnp.ones((8, LANES), F32)
            left = jnp.ones((8, LANES), F32)
            power = a
            for s in range(7):
                tab[2 * c + kind, s] = jnp.where(lane_id >= 2**s, power, 0.0)
                tab[2 * c + kind, 7 + s] = jnp.where(lane_id < LANES - 2**s, power, 0.0)
                right = jnp.where(((lane_id + 1) // 2**s) % 2 == 1, right * power, right)
                left = jnp.where(((LANES - lane_id) // 2**s) % 2 == 1, left * power, left)
                power = power * power
            right = jnp.where(lane_id == LANES - 1, power, right)
            left = jnp.where(lane_id == 0, power, left)
            tab[2 * c + kind, 14] = right
            tab[2 * c + kind, 15] = left
            tab[2 * c + kind, 16] = power
            tab[2 * c + kind, 17] = fwd
            tab[2 * c + kind, 18] = back

    zero = jnp.zeros((half, LANES), F32)
    piece_at = pl.ds(pl.multiple_of(lax.rem(q, 2) * half, half), half)
    a = ax[q // 2, piece_at, :]
    back = gbx[q // 2, piece_at, :]
    f = jnp.ones_like(a)
    states = []
    for c in range(cols):
        f = a * f
        states.append(f)
    cross = zero
    for c in reversed(range(cols)):
        cross = a * cross + back * states[c]
    decay = states[-1]
    square = decay * decay
    total, fade = zero, jnp.ones_like(a)
    for i in range(SPAN):
        total = total + fade
        fade = fade * square
    far_cross = cross * total
    far_decay = jnp.ones_like(a)
    for i in range(SPAN):
        far_decay = far_decay * decay
    carry[0] = decay
    carry[1] = cross
    carry[2] = far_decay
    carry[3] = far_cross

    @pl.loop(1, SPAN)
    def _(d):
        from_span(send_z, recv_z, sz_s, sz_r, d).wait_recv()

    def scan_span(forward, backward):
        decay, cross = carry[0], carry[1]

        def ahead(i, f):
            pre[i] = f
            return recv_z[i, 0].astype(F32) + decay * f

        def behind(k, b):
            i = SPAN - 1 - k
            suf[i] = b
            return recv_z[i, 1].astype(F32) + cross * pre[i] + decay * b

        end = lax.fori_loop(0, SPAN, ahead, forward)
        return end, lax.fori_loop(0, SPAN, behind, backward)

    end, begin = scan_span(zero, zero)
    send_y[0] = end.astype(BF16)
    send_y[1] = begin.astype(BF16)

    def to_group(d):
        peer = lax.rem(y + d, groups)
        return pltpu.make_async_remote_copy(
            src_ref=send_y,
            dst_ref=recv_y.at[y],
            send_sem=sy_s.at[peer],
            recv_sem=sy_r.at[y],
            device_id={"tile": peer * SPAN + q},
            device_id_type=MESH,
        )

    def from_group(d):
        peer = lax.rem(y + d, groups)
        return pltpu.make_async_remote_copy(
            src_ref=send_y,
            dst_ref=recv_y.at[peer],
            send_sem=sy_s.at[peer],
            recv_sem=sy_r.at[peer],
            device_id={"tile": peer * SPAN + q},
            device_id_type=MESH,
        )

    @pl.loop(1, groups)
    def _(d):
        to_group(d).start()

    recv_y[y] = send_y[...]

    @pl.loop(1, groups)
    def _(d):
        from_group(d).wait_recv()

    far_decay, far_cross = carry[2], carry[3]
    enter = []
    f = zero
    mine_f = zero
    for i in range(groups):
        enter.append(f)
        mine_f = jnp.where(y == i, f, mine_f)
        f = recv_y[i, 0].astype(F32) + far_decay * f
    b = zero
    mine_b = zero
    for i in reversed(range(groups)):
        mine_b = jnp.where(y == i, b, mine_b)
        b = recv_y[i, 1].astype(F32) + far_cross * enter[i] + far_decay * b
    scan_span(mine_f, mine_b)

    @pl.loop(0, SPAN)
    def _(i):
        send_c[i, 0] = pre[i].astype(BF16)
        send_c[i, 1] = suf[i].astype(BF16)

    @pl.loop(1, SPAN)
    def _(d):
        to_span(send_c, recv_c, sc_s, sc_r, d).start()

    recv_c[q] = send_c[q]

    @pl.loop(1, SPAN)
    def _(d):
        from_span(send_c, recv_c, sc_s, sc_r, d).wait_recv()

    for b in range(blocks):

        @pl.loop(0, quads)
        def _(p):
            piece = 2 * b + p // per_half
            at = pl.ds(pl.multiple_of(lax.rem(p, per_half) * 16, 16), 16)
            _, backs = local_states(
                b, p, recv_c[piece, 0, at, :].astype(F32), recv_c[piece, 1, at, :].astype(F32)
            )
            dst = pl.ds(pl.multiple_of(p * 16, 16), 16)
            for k in range(own):
                value = backs[k]
                for g in range(1, mems):
                    value = jnp.where(mem == g, backs[g * own + k], value)
                smooth[k, dst, b * LANES : (b + 1) * LANES] = value

    @pl.loop(0, own)
    def _(c):
        @pl.loop(0, padded // 8)
        def _(g):
            t = 2 * c + g // (levels // 8)
            at = pl.ds(pl.multiple_of(g * 8, 8), 8)
            far, fwd, back = tab[t, 16], tab[t, 17], tab[t, 18]
            xs = [fwd * smooth[c, at, b * LANES : (b + 1) * LANES] for b in range(blocks)]
            for s in range(7):
                coeff = tab[t, s]
                xs = [x + coeff * pltpu.roll(x, 2**s, 1) for x in xs]
            reach = tab[t, 14]
            state = jnp.zeros((8, LANES), F32)
            filled = []
            for x in xs:
                filled.append(back * (x + reach * state))
                state = jnp.broadcast_to(x[:, LANES - 1 : LANES], (8, LANES)) + far * state
            xs = filled
            for s in range(7):
                coeff = tab[t, 7 + s]
                xs = [x + coeff * pltpu.roll(x, LANES - 2**s, 1) for x in xs]
            reach = tab[t, 15]
            state = jnp.zeros((8, LANES), F32)
            for b in reversed(range(blocks)):
                x = xs[b]
                smooth[c, at, b * LANES : (b + 1) * LANES] = x + reach * state
                state = jnp.broadcast_to(x[:, 0:1], (8, LANES)) + far * state

    for d in (1, 3, 2):
        send_member(d).wait_recv()
        if d != 2:
            ensemble(recv_m.at[d], False)
    vert_m = vmat[...].astype(BF16)

    @pl.loop(0, own)
    def _(c):
        for w in range(rows // wide_lanes):
            lane = slice(w * wide_lanes, (w + 1) * wide_lanes)
            m = recv_m[2, c, :, lane].astype(F32)
            scaled = (m * own_f[c, :, lane].astype(F32)).astype(BF16)
            term = m * jnp.dot(local_m, scaled, preferred_element_type=F32)
            static = jnp.dot(vert_m, smooth[c, :, lane].astype(BF16), preferred_element_type=F32)
            out[c, :, lane] = (static + (acc[c, :, lane] + term) / (mems - 1)).astype(BF16)

    for d in (2, 1, 3):
        send_member(d).wait_send()

    @pl.loop(1, SPAN)
    def _(d):
        to_span(send_z, recv_z, sz_s, sz_r, d).wait_send()
        to_span(send_c, recv_c, sc_s, sc_r, d).wait_send()

    @pl.loop(1, groups)
    def _(d):
        to_group(d).wait_send()


def body(tiles, mems, field, vert, loc, alpha, xidx, yidx, members):
    slabs, cols, rows = field.shape
    own = cols // mems
    padded = -(-slabs // 16) * 16
    blocks = rows // LANES
    half = padded // 2
    groups = tiles // SPAN
    dma = pltpu.SemaphoreType.DMA
    vmem = pltpu.VMEM
    result = pl.pallas_call(
        functools.partial(kernel, tiles, mems, slabs),
        out_shape=jax.ShapeDtypeStruct((own, padded, rows), BF16),
        in_specs=[pl.BlockSpec(memory_space=pl.ANY)] * 2
        + [pl.BlockSpec(memory_space=pltpu.VMEM)] * 3
        + [pl.BlockSpec(memory_space=pltpu.SMEM)] * 2,
        out_specs=pl.BlockSpec(memory_space=pltpu.VMEM),
        scratch_shapes=[
            vmem((slabs, cols, rows), BF16),
            vmem((slabs, cols, rows), BF16),
            vmem((blocks, padded * cols, LANES), F32),
            vmem((blocks, padded * cols, LANES), F32),
            vmem((mems, own, padded, rows), BF16),
            vmem((mems, own, padded, rows), BF16),
            vmem((own, padded, rows), BF16),
            vmem((blocks, padded, LANES), F32),
            vmem((blocks, padded, LANES), F32),
            vmem((blocks, padded, LANES), F32),
            vmem((SPAN, 2, half, LANES), BF16),
            vmem((SPAN, 2, half, LANES), BF16),
            vmem((SPAN, 2, half, LANES), BF16),
            vmem((SPAN, 2, half, LANES), BF16),
            vmem((2, half, LANES), BF16),
            vmem((groups, 2, half, LANES), BF16),
            vmem((SPAN, half, LANES), F32),
            vmem((SPAN, half, LANES), F32),
            vmem((4, half, LANES), F32),
            vmem((own, padded, rows), F32),
            vmem((own, padded, rows), F32),
            vmem((2 * own, 19, 8, LANES), F32),
            vmem((padded, padded), F32),
            vmem((padded, padded), F32),
            dma((2,)),
            dma((mems,)),
            dma((mems,)),
            dma((SPAN,)),
            dma((SPAN,)),
            dma((SPAN,)),
            dma((SPAN,)),
            dma((groups,)),
            dma((groups,)),
        ],
        compiler_params=pltpu.CompilerParams(
            collective_id=0, has_side_effects=True, vmem_limit_bytes=48 * 2**20
        ),
    )(field, members, vert, loc, xidx, alpha, yidx)
    return jnp.swapaxes(result, 0, 1)[:slabs]


def solution(mesh):
    return jax.shard_map(
        functools.partial(body, mesh.shape["tile"], mesh.shape["mem"]),
        mesh=mesh,
        in_specs=(P(None, "tile", None), P(), P(), P(), P(), P(), P("mem", None, "tile", None)),
        out_specs=P(None, ("tile", "mem"), None),
        check_vma=False,
    )
```

```python
import functools

import jax
import jax.numpy as jnp
from jax import lax
from jax.experimental import pallas as pl
from jax.experimental.pallas import tpu as pltpu
from jax.sharding import PartitionSpec as P

MESH = pl.DeviceIdType.MESH
F32 = jnp.float32
BF16 = jnp.bfloat16
LANES = 128
SPAN = 16


def gains(a):
    return jnp.sqrt(1.0 - a * a), (1.0 - a * a) / jnp.sqrt(1.0 + a * a)


def extended(dst, matrix, pad):
    n = matrix.shape[-1]
    dst[...] = jnp.zeros(dst.shape, F32)
    dst[0:n, 0:n] = matrix[0].astype(F32)
    i = lax.broadcasted_iota(jnp.int32, dst.shape, 0)
    j = lax.broadcasted_iota(jnp.int32, dst.shape, 1)
    keep = (i == j) & (i >= n) & (i < pad)
    dst[...] = jnp.where(keep, 1.0, dst[...])


def kernel(
    tiles, mems, slabs,
    field, members, vert_hbm, loc_hbm, xidx_hbm, alpha_hbm, yidx_hbm,
    out,
    fbuf, mbuf, x32, m32, send_m, recv_m, own_f, ax, gfx, gbx,
    send_z, recv_z, send_c, recv_c, send_y, recv_y, pre, suf, carry,
    lines, weights, mixed, smooth, acc, tab, lmat, vmat, vert, loc, xidx, alpha, yidx,
    local_sem, sm_s, sm_r, sz_s, sz_r, sc_s, sc_r, sy_s, sy_r,
):
    tile = lax.axis_index("tile")
    mem = lax.axis_index("mem")
    groups = tiles // SPAN
    q = lax.rem(tile, SPAN)
    y = tile // SPAN
    cols = field.shape[1]
    rows = field.shape[2]
    blocks = rows // LANES
    own = cols // mems
    levels = vert.shape[-1]
    padded = x32.shape[1] // cols

    get_members = pltpu.make_async_copy(members.at[0], mbuf, local_sem.at[0])
    get_members.start()
    get_field = pltpu.make_async_copy(field, fbuf, local_sem.at[1])
    get_field.start()
    small = [
        pltpu.make_async_copy(src, dst, local_sem.at[2 + at])
        for at, (src, dst) in enumerate(
            (
                (xidx_hbm, xidx),
                (alpha_hbm, alpha),
                (yidx_hbm, yidx),
                (loc_hbm, loc),
                (vert_hbm, vert),
            )
        )
    ]
    for copy in small:
        copy.start()

    barrier = pltpu.get_barrier_semaphore()

    @pl.loop(1, mems)
    def _(d):
        pl.semaphore_signal(
            barrier, inc=1, device_id={"mem": lax.rem(mem + d, mems)}, device_id_type=MESH
        )

    @pl.loop(1, SPAN)
    def _(d):
        pl.semaphore_signal(
            barrier,
            inc=1,
            device_id={"tile": y * SPAN + lax.rem(q + d, SPAN)},
            device_id_type=MESH,
        )

    @pl.loop(1, groups)
    def _(d):
        pl.semaphore_signal(
            barrier,
            inc=1,
            device_id={"tile": lax.rem(y + d, groups) * SPAN + q},
            device_id_type=MESH,
        )

    for copy in small:
        copy.wait()
    sub = lax.broadcasted_iota(jnp.int32, (padded, LANES), 0)

    @pl.loop(0, blocks)
    def _(b):
        lane = pl.ds(pl.multiple_of(b * LANES, LANES), LANES)
        idx = xidx[:, lane]
        a = jnp.zeros(idx.shape, F32)
        for k in range(alpha.shape[0]):
            a = jnp.where(idx == k, alpha[k], a)
        wide = jnp.where(
            sub < levels,
            jnp.broadcast_to(a[0:1], (padded, LANES)),
            jnp.broadcast_to(a[1:2], (padded, LANES)),
        )
        fwd, back = gains(wide)
        ax[b] = wide
        gfx[b] = fwd
        gbx[b] = back

    extended(lmat, loc, slabs)
    extended(vmat, vert, slabs)

    def spread(src, dst):
        for b in range(blocks):
            dst[b, pl.ds(slabs * cols, (padded - slabs) * cols), :] = jnp.zeros(
                ((padded - slabs) * cols, LANES), F32
            )

        @pl.loop(0, slabs)
        def _(s):
            at = pl.ds(pl.multiple_of(s * cols, cols), cols)
            for b in range(blocks):
                dst[b, at, :] = src[s, :, b * LANES : (b + 1) * LANES].astype(F32)

    def send_member(d):
        return pltpu.make_async_remote_copy(
            src_ref=send_m.at[lax.rem(mem + d, mems)],
            dst_ref=recv_m.at[d],
            send_sem=sm_s.at[d],
            recv_sem=sm_r.at[d],
            device_id={"mem": lax.rem(mem + d, mems)},
            device_id_type=MESH,
        )

    def collect(src, dst, first):
        @pl.loop(0, own)
        def _(c):
            for b in range(blocks):
                part = src[b, pl.ds(first + c, padded, stride=cols), :]
                dst[c, :, b * LANES : (b + 1) * LANES] = part.astype(BF16)

    get_members.wait()
    spread(mbuf, m32)
    collect(m32, send_m.at[lax.rem(mem + 2, mems)], lax.rem(mem + 2, mems) * own)
    pl.semaphore_wait(barrier, (mems - 1) + (SPAN - 1) + (groups - 1))
    send_member(2).start()
    for d in (1, 3):
        peer = lax.rem(mem + d, mems)
        collect(m32, send_m.at[peer], peer * own)
        send_member(d).start()

    get_field.wait()
    spread(fbuf, x32)

    quads = padded // 16
    half = padded // 2
    per_half = half // 16

    def local_states(b, p, f, start):
        at = pl.ds(pl.multiple_of(p * 16, 16), 16)
        a, fwd, back = ax[b, at, :], gfx[b, at, :], gbx[b, at, :]
        states = []
        for c in range(cols):
            f = a * f + fwd * x32[b, pl.ds(p * 16 * cols + c, 16, stride=cols), :]
            states.append(f)
        value = start
        backs = [None] * cols
        for c in reversed(range(cols)):
            value = a * value + back * states[c]
            backs[c] = value
        return states, backs

    @pl.loop(0, blocks)
    def _(b):
        @pl.loop(0, quads)
        def _(p):
            zero = jnp.zeros((16, LANES), F32)
            states, backs = local_states(b, p, zero, zero)
            piece = 2 * b + p // per_half
            at = pl.ds(pl.multiple_of(lax.rem(p, per_half) * 16, 16), 16)
            send_z[piece, 0, at, :] = states[-1].astype(BF16)
            send_z[piece, 1, at, :] = backs[0].astype(BF16)

    def to_span(src, dst, s_sem, r_sem, d):
        peer = lax.rem(q + d, SPAN)
        return pltpu.make_async_remote_copy(
            src_ref=src.at[peer],
            dst_ref=dst.at[q],
            send_sem=s_sem.at[peer],
            recv_sem=r_sem.at[q],
            device_id={"tile": y * SPAN + peer},
            device_id_type=MESH,
        )

    def from_span(src, dst, s_sem, r_sem, d):
        peer = lax.rem(q + d, SPAN)
        return pltpu.make_async_remote_copy(
            src_ref=src.at[peer],
            dst_ref=dst.at[peer],
            send_sem=s_sem.at[peer],
            recv_sem=r_sem.at[peer],
            device_id={"tile": y * SPAN + peer},
            device_id_type=MESH,
        )

    @pl.loop(1, SPAN)
    def _(d):
        to_span(send_z, recv_z, sz_s, sz_r, d).start()

    recv_z[q] = send_z[q]

    collect(m32, send_m.at[mem], mem * own)
    collect(x32, own_f, mem * own)

    wide_lanes = 2 * LANES
    local_m = lmat[...].astype(BF16)

    def ensemble(src, first):
        @pl.loop(0, own)
        def _(c):
            for w in range(rows // wide_lanes):
                lane = slice(w * wide_lanes, (w + 1) * wide_lanes)
                m = src[c, :, lane].astype(F32)
                scaled = (m * own_f[c, :, lane].astype(F32)).astype(BF16)
                term = m * jnp.dot(local_m, scaled, preferred_element_type=F32)
                acc[c, :, lane] = term if first else acc[c, :, lane] + term

    ensemble(send_m.at[mem], True)

    lane8 = lax.broadcasted_iota(jnp.int32, (8, LANES), 1)
    sub8 = lax.broadcasted_iota(jnp.int32, (8, LANES), 0)
    row_i = lax.broadcasted_iota(jnp.int32, (LANES, LANES), 0)
    row_j = lax.broadcasted_iota(jnp.int32, (LANES, LANES), 1)

    def geometric(count, ratio):
        value = jnp.zeros(count.shape, F32)
        reached = jnp.ones(count.shape, F32)
        part = jnp.float32(1.0)
        for bit in range(8):
            has = (count & (1 << bit)) != 0
            value = jnp.where(has, value + reached * part, value)
            reached = jnp.where(has, reached * ratio, reached)
            part = part * (1.0 + ratio)
            ratio = ratio * ratio
        return value

    @pl.loop(0, own)
    def _(c):
        col = tile * cols + mem * own + c
        tables = []
        for kind in range(2):
            coeff = alpha[yidx[kind, col]]
            a = jnp.full((8, LANES), coeff, F32)
            fwd, back = gains(a)
            rate = jnp.log(jnp.maximum(a, 1e-37))

            def tall(x):
                return jnp.broadcast_to(x[0:1], (LANES, LANES))

            def power(exponent, log_a):
                return jnp.exp(exponent.astype(F32) * log_a)

            ratio = coeff * coeff
            inner = power(jnp.abs(row_i - row_j), tall(rate)) * tall(fwd * back)
            inner = inner * geometric(LANES - jnp.maximum(row_i, row_j), ratio)
            ends = power(LANES - 1 - row_i, tall(rate)) * tall(fwd)
            starts = jnp.broadcast_to(inner[:, 0:1], (LANES, LANES))
            for at, part in enumerate((inner, ends, starts)):
                high = part.astype(BF16)
                low = (part - high.astype(F32)).astype(BF16)
                lane = slice(at * LANES, (at + 1) * LANES)
                weights[2 * c + kind, 0:LANES, lane] = high
                weights[2 * c + kind, LANES : 2 * LANES, lane] = low
            far = coeff
            for _ in range(7):
                far = far * far
            whole = geometric(jnp.full((8, LANES), LANES, jnp.int32), ratio)
            tables.append(
                (
                    back * power(lane8 + 1, rate) * geometric(LANES - lane8, ratio),
                    power(LANES - lane8, rate),
                    jnp.full((8, LANES), far, F32),
                    back * a * whole,
                )
            )
        for at, (first, second) in enumerate(zip(*tables)):
            tab[2 * c, at] = first
            tab[2 * c + 1, at] = jnp.where(sub8 < levels % 8, first, second)

    zero = jnp.zeros((half, LANES), F32)
    piece_at = pl.ds(pl.multiple_of(lax.rem(q, 2) * half, half), half)
    a = ax[q // 2, piece_at, :]
    back = gbx[q // 2, piece_at, :]
    f = jnp.ones_like(a)
    states = []
    for c in range(cols):
        f = a * f
        states.append(f)
    cross = zero
    for c in reversed(range(cols)):
        cross = a * cross + back * states[c]
    decay = states[-1]
    square = decay * decay
    total, fade = zero, jnp.ones_like(a)
    for i in range(SPAN):
        total = total + fade
        fade = fade * square
    far_cross = cross * total
    far_decay = jnp.ones_like(a)
    for i in range(SPAN):
        far_decay = far_decay * decay
    carry[0] = decay
    carry[1] = cross
    carry[2] = far_decay
    carry[3] = far_cross

    @pl.loop(1, SPAN)
    def _(d):
        from_span(send_z, recv_z, sz_s, sz_r, d).wait_recv()

    def scan_span(forward, backward):
        decay, cross = carry[0], carry[1]

        def ahead(i, f):
            pre[i] = f
            return recv_z[i, 0].astype(F32) + decay * f

        def behind(k, b):
            i = SPAN - 1 - k
            suf[i] = b
            return recv_z[i, 1].astype(F32) + cross * pre[i] + decay * b

        end = lax.fori_loop(0, SPAN, ahead, forward)
        return end, lax.fori_loop(0, SPAN, behind, backward)

    end, begin = scan_span(zero, zero)
    send_y[0] = end.astype(BF16)
    send_y[1] = begin.astype(BF16)

    def to_group(d):
        peer = lax.rem(y + d, groups)
        return pltpu.make_async_remote_copy(
            src_ref=send_y,
            dst_ref=recv_y.at[y],
            send_sem=sy_s.at[peer],
            recv_sem=sy_r.at[y],
            device_id={"tile": peer * SPAN + q},
            device_id_type=MESH,
        )

    def from_group(d):
        peer = lax.rem(y + d, groups)
        return pltpu.make_async_remote_copy(
            src_ref=send_y,
            dst_ref=recv_y.at[peer],
            send_sem=sy_s.at[peer],
            recv_sem=sy_r.at[peer],
            device_id={"tile": peer * SPAN + q},
            device_id_type=MESH,
        )

    @pl.loop(1, groups)
    def _(d):
        to_group(d).start()

    recv_y[y] = send_y[...]

    @pl.loop(1, groups)
    def _(d):
        from_group(d).wait_recv()

    far_decay, far_cross = carry[2], carry[3]
    enter = []
    f = zero
    mine_f = zero
    for i in range(groups):
        enter.append(f)
        mine_f = jnp.where(y == i, f, mine_f)
        f = recv_y[i, 0].astype(F32) + far_decay * f
    b = zero
    mine_b = zero
    for i in reversed(range(groups)):
        mine_b = jnp.where(y == i, b, mine_b)
        b = recv_y[i, 1].astype(F32) + far_cross * enter[i] + far_decay * b
    scan_span(mine_f, mine_b)

    @pl.loop(0, SPAN)
    def _(i):
        send_c[i, 0] = pre[i].astype(BF16)
        send_c[i, 1] = suf[i].astype(BF16)

    @pl.loop(1, SPAN)
    def _(d):
        to_span(send_c, recv_c, sc_s, sc_r, d).start()

    recv_c[q] = send_c[q]

    @pl.loop(1, SPAN)
    def _(d):
        from_span(send_c, recv_c, sc_s, sc_r, d).wait_recv()

    for b in range(blocks):

        @pl.loop(0, quads)
        def _(p):
            piece = 2 * b + p // per_half
            at = pl.ds(pl.multiple_of(lax.rem(p, per_half) * 16, 16), 16)
            _, backs = local_states(
                b, p, recv_c[piece, 0, at, :].astype(F32), recv_c[piece, 1, at, :].astype(F32)
            )
            dst = pl.ds(pl.multiple_of(b * padded + p * 16, 16), 16)
            for k in range(own):
                value = backs[k]
                for g in range(1, mems):
                    value = jnp.where(mem == g, backs[g * own + k], value)
                lines[k, dst, :] = value.astype(BF16)

    last = padded - 8

    @pl.loop(0, own)
    def _(c):
        x = jnp.concatenate([lines[c], lines[c]], axis=1)
        mixed[...] = jnp.dot(x, weights[2 * c], preferred_element_type=F32)
        for b in range(blocks):
            at = slice(b * padded + padded - 16, (b + 1) * padded)
            x = jnp.concatenate([lines[c, at, :], lines[c, at, :]], axis=1)
            other = jnp.dot(x, weights[2 * c + 1], preferred_element_type=F32)[8:]
            at = slice(b * padded + last, (b + 1) * padded)
            pick = jnp.concatenate([sub8] * 3, axis=1) < levels % 8
            mixed[at, :] = jnp.where(pick, mixed[at, :], other)

        @pl.loop(0, padded // 8)
        def _(g):
            t = 2 * c + g // (levels // 8)
            from_left, from_right, far, cross = tab[t, 0], tab[t, 1], tab[t, 2], tab[t, 3]

            def block(b, part):
                at = pl.ds(pl.multiple_of(b * padded + g * 8, 8), 8)
                return mixed[at, part * LANES : (part + 1) * LANES]

            state = jnp.zeros((8, LANES), F32)
            entering = []
            for b in range(blocks):
                entering.append(state)
                state = block(b, 1) + far * state
            state = jnp.zeros((8, LANES), F32)
            for b in reversed(range(blocks)):
                value = block(b, 0) + from_left * entering[b] + from_right * state
                smooth[c, pl.ds(pl.multiple_of(g * 8, 8), 8), b * LANES : (b + 1) * LANES] = value
                state = block(b, 2) + cross * entering[b] + far * state

    for d in (1, 3, 2):
        send_member(d).wait_recv()
        if d != 2:
            ensemble(recv_m.at[d], False)
    vert_m = vmat[...].astype(BF16)

    @pl.loop(0, own)
    def _(c):
        for w in range(rows // wide_lanes):
            lane = slice(w * wide_lanes, (w + 1) * wide_lanes)
            m = recv_m[2, c, :, lane].astype(F32)
            scaled = (m * own_f[c, :, lane].astype(F32)).astype(BF16)
            term = m * jnp.dot(local_m, scaled, preferred_element_type=F32)
            static = jnp.dot(vert_m, smooth[c, :, lane].astype(BF16), preferred_element_type=F32)
            out[c, :, lane] = (static + (acc[c, :, lane] + term) / (mems - 1)).astype(BF16)

    for d in (2, 1, 3):
        send_member(d).wait_send()

    @pl.loop(1, SPAN)
    def _(d):
        to_span(send_z, recv_z, sz_s, sz_r, d).wait_send()
        to_span(send_c, recv_c, sc_s, sc_r, d).wait_send()

    @pl.loop(1, groups)
    def _(d):
        to_group(d).wait_send()


def body(tiles, mems, field, vert, loc, alpha, xidx, yidx, members):
    slabs, cols, rows = field.shape
    own = cols // mems
    padded = -(-slabs // 16) * 16
    blocks = rows // LANES
    half = padded // 2
    groups = tiles // SPAN
    dma = pltpu.SemaphoreType.DMA
    vmem = pltpu.VMEM
    result = pl.pallas_call(
        functools.partial(kernel, tiles, mems, slabs),
        out_shape=jax.ShapeDtypeStruct((own, padded, rows), BF16),
        in_specs=[pl.BlockSpec(memory_space=pl.ANY)] * 7,
        out_specs=pl.BlockSpec(memory_space=pltpu.VMEM),
        scratch_shapes=[
            vmem((slabs, cols, rows), BF16),
            vmem((slabs, cols, rows), BF16),
            vmem((blocks, padded * cols, LANES), F32),
            vmem((blocks, padded * cols, LANES), F32),
            vmem((mems, own, padded, rows), BF16),
            vmem((mems, own, padded, rows), BF16),
            vmem((own, padded, rows), BF16),
            vmem((blocks, padded, LANES), F32),
            vmem((blocks, padded, LANES), F32),
            vmem((blocks, padded, LANES), F32),
            vmem((SPAN, 2, half, LANES), BF16),
            vmem((SPAN, 2, half, LANES), BF16),
            vmem((SPAN, 2, half, LANES), BF16),
            vmem((SPAN, 2, half, LANES), BF16),
            vmem((2, half, LANES), BF16),
            vmem((groups, 2, half, LANES), BF16),
            vmem((SPAN, half, LANES), F32),
            vmem((SPAN, half, LANES), F32),
            vmem((4, half, LANES), F32),
            vmem((own, blocks * padded, LANES), BF16),
            vmem((2 * own, 2 * LANES, 3 * LANES), BF16),
            vmem((blocks * padded, 3 * LANES), F32),
            vmem((own, padded, rows), F32),
            vmem((own, padded, rows), F32),
            vmem((2 * own, 4, 8, LANES), F32),
            vmem((padded, padded), F32),
            vmem((padded, padded), F32),
            vmem(vert.shape, vert.dtype),
            vmem(loc.shape, loc.dtype),
            vmem(xidx.shape, xidx.dtype),
            pltpu.SMEM(alpha.shape, alpha.dtype),
            pltpu.SMEM(yidx.shape, yidx.dtype),
            dma((7,)),
            dma((mems,)),
            dma((mems,)),
            dma((SPAN,)),
            dma((SPAN,)),
            dma((SPAN,)),
            dma((SPAN,)),
            dma((groups,)),
            dma((groups,)),
        ],
        compiler_params=pltpu.CompilerParams(
            collective_id=0, has_side_effects=True, vmem_limit_bytes=60 * 2**20
        ),
    )(field, members, vert, loc, xidx, alpha, yidx)
    return jnp.swapaxes(result, 0, 1)[:slabs]


def solution(mesh):
    return jax.shard_map(
        functools.partial(body, mesh.shape["tile"], mesh.shape["mem"]),
        mesh=mesh,
        in_specs=(P(None, "tile", None), P(), P(), P(), P(), P(), P("mem", None, "tile", None)),
        out_specs=P(None, ("tile", "mem"), None),
        check_vma=False,
    )
```

```python
import functools

import jax
import jax.numpy as jnp
from jax import lax
from jax.experimental import pallas as pl
from jax.experimental.pallas import tpu as pltpu
from jax.sharding import PartitionSpec as P

MESH = pl.DeviceIdType.MESH
F32 = jnp.float32
BF16 = jnp.bfloat16
LANES = 128
SPAN = 16


def gains(a):
    return jnp.sqrt(1.0 - a * a), (1.0 - a * a) / jnp.sqrt(1.0 + a * a)


def extended(dst, matrix, pad):
    n = matrix.shape[-1]
    dst[...] = jnp.zeros(dst.shape, F32)
    dst[0:n, 0:n] = matrix[0].astype(F32)
    i = lax.broadcasted_iota(jnp.int32, dst.shape, 0)
    j = lax.broadcasted_iota(jnp.int32, dst.shape, 1)
    keep = (i == j) & (i >= n) & (i < pad)
    dst[...] = jnp.where(keep, 1.0, dst[...])


def kernel(
    tiles, mems, slabs,
    field, members, vert_hbm, loc_hbm, xidx_hbm, alpha_hbm, yidx_hbm,
    out,
    fbuf, mbuf, x32, m32, send_m, recv_m, own_f, ax, gfx, gbx,
    send_z, recv_z, send_c, entering_all, send_y, recv_y, base, reach,
    lines, weights, mixed, smooth, acc, tab, lmat, vmat, vert, loc, xidx, alpha, yidx,
    local_sem, sm_s, sm_r, sz_s, sz_r, sc_s, sc_r, sy_s, sy_r, sx_s, sx_r,
):
    tile = lax.axis_index("tile")
    mem = lax.axis_index("mem")
    groups = tiles // SPAN
    q = lax.rem(tile, SPAN)
    y = tile // SPAN
    cols = field.shape[1]
    rows = field.shape[2]
    blocks = rows // LANES
    own = cols // mems
    levels = vert.shape[-1]
    padded = x32.shape[1] // cols

    get_field = pltpu.make_async_copy(field, fbuf, local_sem.at[1])
    get_field.start()
    small = [
        pltpu.make_async_copy(src, dst, local_sem.at[2 + at])
        for at, (src, dst) in enumerate(
            (
                (xidx_hbm, xidx),
                (alpha_hbm, alpha),
                (yidx_hbm, yidx),
                (loc_hbm, loc),
                (vert_hbm, vert),
            )
        )
    ]
    for copy in small:
        copy.start()
    get_members = pltpu.make_async_copy(members.at[0], mbuf, local_sem.at[0])
    get_members.start()

    barrier = pltpu.get_barrier_semaphore()

    @pl.loop(1, mems)
    def _(d):
        pl.semaphore_signal(
            barrier, inc=1, device_id={"mem": lax.rem(mem + d, mems)}, device_id_type=MESH
        )

    @pl.loop(1, SPAN)
    def _(d):
        pl.semaphore_signal(
            barrier,
            inc=1,
            device_id={"tile": y * SPAN + lax.rem(q + d, SPAN)},
            device_id_type=MESH,
        )

    @pl.loop(1, groups)
    def _(d):
        pl.semaphore_signal(
            barrier,
            inc=1,
            device_id={"tile": lax.rem(y + d, groups) * SPAN + q},
            device_id_type=MESH,
        )

    for copy in small:
        copy.wait()
    sub = lax.broadcasted_iota(jnp.int32, (padded, LANES), 0)

    @pl.loop(0, blocks)
    def _(b):
        lane = pl.ds(pl.multiple_of(b * LANES, LANES), LANES)
        idx = xidx[:, lane]
        a = jnp.zeros(idx.shape, F32)
        for k in range(alpha.shape[0]):
            a = jnp.where(idx == k, alpha[k], a)
        wide = jnp.where(
            sub < levels,
            jnp.broadcast_to(a[0:1], (padded, LANES)),
            jnp.broadcast_to(a[1:2], (padded, LANES)),
        )
        fwd, back = gains(wide)
        ax[b] = wide
        gfx[b] = fwd
        gbx[b] = back

    def spread(src, dst):
        for b in range(blocks):
            dst[b, pl.ds(slabs * cols, (padded - slabs) * cols), :] = jnp.zeros(
                ((padded - slabs) * cols, LANES), F32
            )

        @pl.loop(0, slabs)
        def _(s):
            at = pl.ds(pl.multiple_of(s * cols, cols), cols)
            for b in range(blocks):
                dst[b, at, :] = src[s, :, b * LANES : (b + 1) * LANES].astype(F32)

    def send_member(d):
        return pltpu.make_async_remote_copy(
            src_ref=send_m.at[lax.rem(mem + d, mems)],
            dst_ref=recv_m.at[d],
            send_sem=sm_s.at[d],
            recv_sem=sm_r.at[d],
            device_id={"mem": lax.rem(mem + d, mems)},
            device_id_type=MESH,
        )

    def collect(src, dst, first):
        @pl.loop(0, own)
        def _(c):
            for b in range(blocks):
                part = src[b, pl.ds(first + c, padded, stride=cols), :]
                dst[c, :, b * LANES : (b + 1) * LANES] = part.astype(BF16)

    quads = padded // 16

    def local_states(b, p):
        at = pl.ds(pl.multiple_of(p * 16, 16), 16)
        a, fwd, back = ax[b, at, :], gfx[b, at, :], gbx[b, at, :]
        f = jnp.zeros((16, LANES), F32)
        states = []
        for c in range(cols):
            f = a * f + fwd * x32[b, pl.ds(p * 16 * cols + c, 16, stride=cols), :]
            states.append(f)
        value = jnp.zeros((16, LANES), F32)
        backs = [None] * cols
        for c in reversed(range(cols)):
            value = a * value + back * states[c]
            backs[c] = value
        return states, backs

    def mine(values, k):
        value = values[k]
        for g in range(1, mems):
            value = jnp.where(mem == g, values[g * own + k], value)
        return value

    def to_span(src, dst, s_sem, r_sem, d):
        peer = lax.rem(q + d, SPAN)
        return pltpu.make_async_remote_copy(
            src_ref=src.at[peer],
            dst_ref=dst.at[q],
            send_sem=s_sem.at[peer],
            recv_sem=r_sem.at[q],
            device_id={"tile": y * SPAN + peer},
            device_id_type=MESH,
        )

    def from_span(src, dst, s_sem, r_sem, d):
        peer = lax.rem(q + d, SPAN)
        return pltpu.make_async_remote_copy(
            src_ref=src.at[peer],
            dst_ref=dst.at[peer],
            send_sem=s_sem.at[peer],
            recv_sem=r_sem.at[peer],
            device_id={"tile": y * SPAN + peer},
            device_id_type=MESH,
        )

    get_field.wait()
    spread(fbuf, x32)

    @pl.loop(0, blocks)
    def _(b):
        states, backs = local_states(b, mem)
        for h in range(2):
            part = slice(8 * h, 8 * h + 8)
            pair = jnp.concatenate([states[-1][part], backs[0][part]], axis=0)
            send_z[2 * b + h] = pair.astype(BF16)

    pl.semaphore_wait(barrier, (mems - 1) + (SPAN - 1) + (groups - 1))

    @pl.loop(1, SPAN)
    def _(d):
        to_span(send_z, recv_z, sz_s, sz_r, d).start()

    recv_z[q] = send_z[q]

    get_members.wait()
    spread(mbuf, m32)
    for d in (2, 1, 3):
        peer = lax.rem(mem + d, mems)
        collect(m32, send_m.at[peer], peer * own)
        send_member(d).start()

    zero = jnp.zeros((8, LANES), F32)
    piece_at = pl.ds(pl.multiple_of(mem * 16 + lax.rem(q, 2) * 8, 8), 8)
    a = ax[q // 2, piece_at, :]
    back = gbx[q // 2, piece_at, :]
    f = jnp.ones_like(a)
    states = []
    for c in range(cols):
        f = a * f
        states.append(f)
    cross = zero
    for c in reversed(range(cols)):
        cross = a * cross + back * states[c]
    decay = states[-1]
    square = decay * decay
    total, fade, far_decay = zero, jnp.ones_like(a), jnp.ones_like(a)
    for _ in range(SPAN):
        total = total + fade
        fade = fade * square
        far_decay = far_decay * decay
    far_cross = cross * total

    @pl.loop(1, SPAN)
    def _(d):
        from_span(send_z, recv_z, sz_s, sz_r, d).wait_recv()

    def scan_span(f, b):
        enter_f, enter_b = [], [None] * SPAN
        pairs = [recv_z[i].astype(F32) for i in range(SPAN)]
        for i in range(SPAN):
            enter_f.append(f)
            f = pairs[i][0:8] + decay * f
        for i in reversed(range(SPAN)):
            enter_b[i] = b
            b = pairs[i][8:16] + cross * enter_f[i] + decay * b
        return f, b, enter_f, enter_b

    end, begin, _, _ = scan_span(zero, zero)
    send_y[...] = jnp.concatenate([end, begin], axis=0).astype(BF16)

    def to_group(d):
        peer = lax.rem(y + d, groups)
        return pltpu.make_async_remote_copy(
            src_ref=send_y,
            dst_ref=recv_y.at[y],
            send_sem=sy_s.at[peer],
            recv_sem=sy_r.at[y],
            device_id={"tile": peer * SPAN + q},
            device_id_type=MESH,
        )

    def from_group(d):
        peer = lax.rem(y + d, groups)
        return pltpu.make_async_remote_copy(
            src_ref=send_y,
            dst_ref=recv_y.at[peer],
            send_sem=sy_s.at[peer],
            recv_sem=sy_r.at[peer],
            device_id={"tile": peer * SPAN + q},
            device_id_type=MESH,
        )

    @pl.loop(1, groups)
    def _(d):
        to_group(d).start()

    recv_y[y] = send_y[...]

    @pl.loop(0, blocks)
    def _(b):
        @pl.loop(0, quads)
        def _(p):
            _, backs = local_states(b, p)
            at = pl.ds(pl.multiple_of(b * padded + p * 16, 16), 16)
            for k in range(own):
                base[k, at, :] = mine(backs, k)

        for kind in range(2):
            at = slice(0, 16) if kind == 0 else slice(padded - 16, padded)
            a, back = ax[b, at, :], gbx[b, at, :]
            f = jnp.ones((16, LANES), F32)
            states = []
            for c in range(cols):
                f = a * f
                states.append(f)
            value = jnp.zeros((16, LANES), F32)
            backs = [None] * cols
            for c in reversed(range(cols)):
                value = a * value + back * states[c]
                backs[c] = value
            for k in range(own):
                reach[kind, b, 2 * k] = mine(backs, k)
                reach[kind, b, 2 * k + 1] = mine(states[::-1], k)

    @pl.loop(1, groups)
    def _(d):
        from_group(d).wait_recv()

    pairs = [recv_y[i].astype(F32) for i in range(groups)]
    enter = []
    f = zero
    mine_f = zero
    for i in range(groups):
        enter.append(f)
        mine_f = jnp.where(y == i, f, mine_f)
        f = pairs[i][0:8] + far_decay * f
    b = zero
    mine_b = zero
    for i in reversed(range(groups)):
        mine_b = jnp.where(y == i, b, mine_b)
        b = pairs[i][8:16] + far_cross * enter[i] + far_decay * b
    _, _, enter_f, enter_b = scan_span(mine_f, mine_b)
    for i in range(SPAN):
        send_c[i] = jnp.concatenate([enter_f[i], enter_b[i]], axis=0).astype(BF16)

    recv_c = entering_all.at[mem]

    @pl.loop(1, SPAN)
    def _(d):
        to_span(send_c, recv_c, sc_s, sc_r, d).start()

    entering_all[mem, q] = send_c[q]

    wide_lanes = 2 * LANES
    def ensemble(src, first):
        @pl.loop(0, own)
        def _(c):
            for w in range(rows // wide_lanes):
                lane = slice(w * wide_lanes, (w + 1) * wide_lanes)
                m = src[c, :, lane].astype(F32)
                scaled = (m * own_f[c, :, lane].astype(F32)).astype(BF16)
                term = m * jnp.dot(local_m, scaled, preferred_element_type=F32)
                acc[c, :, lane] = term if first else acc[c, :, lane] + term

    collect(m32, send_m.at[mem], mem * own)
    collect(x32, own_f, mem * own)
    extended(lmat, loc, slabs)
    extended(vmat, vert, slabs)

    local_m = lmat[...].astype(BF16)
    ensemble(send_m.at[mem], True)

    @pl.loop(1, SPAN)
    def _(d):
        from_span(send_c, recv_c, sc_s, sc_r, d).wait_recv()

    def gather(d):
        return pltpu.make_async_remote_copy(
            src_ref=entering_all.at[mem],
            dst_ref=entering_all.at[mem],
            send_sem=sx_s.at[d],
            recv_sem=sx_r.at[d],
            device_id={"mem": lax.rem(mem + d, mems)},
            device_id_type=MESH,
        )

    def gathered(d):
        peer = lax.rem(mem + mems - d, mems)
        return pltpu.make_async_remote_copy(
            src_ref=entering_all.at[peer],
            dst_ref=entering_all.at[peer],
            send_sem=sx_s.at[d],
            recv_sem=sx_r.at[d],
            device_id={"mem": lax.rem(mem + d, mems)},
            device_id_type=MESH,
        )

    for d in (2, 1, 3):
        gather(d).start()

    lane8 = lax.broadcasted_iota(jnp.int32, (8, LANES), 1)
    sub8 = lax.broadcasted_iota(jnp.int32, (8, LANES), 0)
    row_i = lax.broadcasted_iota(jnp.int32, (LANES, LANES), 0)
    row_j = lax.broadcasted_iota(jnp.int32, (LANES, LANES), 1)

    def geometric(count, ratio):
        value = jnp.zeros(count.shape, F32)
        reached = jnp.ones(count.shape, F32)
        part = jnp.float32(1.0)
        for bit in range(8):
            has = (count & (1 << bit)) != 0
            value = jnp.where(has, value + reached * part, value)
            reached = jnp.where(has, reached * ratio, reached)
            part = part * (1.0 + ratio)
            ratio = ratio * ratio
        return value

    @pl.loop(0, own)
    def _(c):
        col = tile * cols + mem * own + c
        tables = []
        for kind in range(2):
            coeff = alpha[yidx[kind, col]]
            a = jnp.full((8, LANES), coeff, F32)
            fwd, back = gains(a)
            rate = jnp.log(jnp.maximum(a, 1e-37))

            def tall(x):
                return jnp.broadcast_to(x[0:1], (LANES, LANES))

            def power(exponent, log_a):
                return jnp.exp(exponent.astype(F32) * log_a)

            ratio = coeff * coeff
            inner = power(jnp.abs(row_i - row_j), tall(rate)) * tall(fwd * back)
            inner = inner * geometric(LANES - jnp.maximum(row_i, row_j), ratio)
            ends = power(LANES - 1 - row_i, tall(rate)) * tall(fwd)
            starts = jnp.broadcast_to(inner[:, 0:1], (LANES, LANES))
            for at, part in enumerate((inner, ends, starts)):
                high = part.astype(BF16)
                low = (part - high.astype(F32)).astype(BF16)
                lane = slice(at * LANES, (at + 1) * LANES)
                weights[2 * c + kind, 0:LANES, lane] = high
                weights[2 * c + kind, LANES : 2 * LANES, lane] = low
            far = coeff
            for _ in range(7):
                far = far * far
            whole = geometric(jnp.full((8, LANES), LANES, jnp.int32), ratio)
            tables.append(
                (
                    back * power(lane8 + 1, rate) * geometric(LANES - lane8, ratio),
                    power(LANES - lane8, rate),
                    jnp.full((8, LANES), far, F32),
                    back * a * whole,
                )
            )
        for at, (first, second) in enumerate(zip(*tables)):
            tab[2 * c, at] = first
            tab[2 * c + 1, at] = jnp.where(sub8 < levels % 8, first, second)

    for d in (1, 3, 2):
        gathered(d).wait_recv()

    @pl.loop(0, quads)
    def _(p):
        kind = p // (quads - 1)

        @pl.loop(0, blocks)
        def _(b):
            low = entering_all[p, 2 * b].astype(F32)
            high = entering_all[p, 2 * b + 1].astype(F32)
            f = jnp.concatenate([low[0:8], high[0:8]], axis=0)
            bk = jnp.concatenate([low[8:16], high[8:16]], axis=0)
            at = pl.ds(pl.multiple_of(b * padded + p * 16, 16), 16)
            for k in range(own):
                value = base[k, at, :] + reach[kind, b, 2 * k] * f + reach[kind, b, 2 * k + 1] * bk
                lines[k, at, :] = value.astype(BF16)

    last = padded - 8

    @pl.loop(0, own)
    def _(c):
        x = jnp.concatenate([lines[c], lines[c]], axis=1)
        mixed[...] = jnp.dot(x, weights[2 * c], preferred_element_type=F32)
        tail = jnp.concatenate(
            [lines[c, (b + 1) * padded - 16 : (b + 1) * padded, :] for b in range(blocks)], axis=0
        )
        tail = jnp.concatenate([tail, tail], axis=1)
        other = jnp.dot(tail, weights[2 * c + 1], preferred_element_type=F32)
        pick = jnp.concatenate([sub8] * 3, axis=1) < levels % 8
        for b in range(blocks):
            at = slice(b * padded + last, (b + 1) * padded)
            mixed[at, :] = jnp.where(pick, mixed[at, :], other[16 * b + 8 : 16 * b + 16])

        for g in range(padded // 8):
            t = 2 * c + g // (levels // 8)
            from_left, from_right, far, cross = tab[t, 0], tab[t, 1], tab[t, 2], tab[t, 3]

            def block(b, part):
                at = slice(b * padded + g * 8, b * padded + g * 8 + 8)
                return mixed[at, part * LANES : (part + 1) * LANES]

            state = jnp.zeros((8, LANES), F32)
            entering = []
            for b in range(blocks):
                entering.append(state)
                state = block(b, 1) + far * state
            state = jnp.zeros((8, LANES), F32)
            for b in reversed(range(blocks)):
                value = block(b, 0) + from_left * entering[b] + from_right * state
                smooth[c, g * 8 : g * 8 + 8, b * LANES : (b + 1) * LANES] = value
                state = block(b, 2) + cross * entering[b] + far * state

    for d in (1, 3, 2):
        send_member(d).wait_recv()
        if d != 2:
            ensemble(recv_m.at[d], False)
    vert_m = vmat[...].astype(BF16)

    @pl.loop(0, own)
    def _(c):
        for w in range(rows // wide_lanes):
            lane = slice(w * wide_lanes, (w + 1) * wide_lanes)
            m = recv_m[2, c, :, lane].astype(F32)
            scaled = (m * own_f[c, :, lane].astype(F32)).astype(BF16)
            term = m * jnp.dot(local_m, scaled, preferred_element_type=F32)
            static = jnp.dot(vert_m, smooth[c, :, lane].astype(BF16), preferred_element_type=F32)
            out[c, :, lane] = (static + (acc[c, :, lane] + term) / (mems - 1)).astype(BF16)

    for d in (2, 1, 3):
        send_member(d).wait_send()
        gather(d).wait_send()

    @pl.loop(1, SPAN)
    def _(d):
        to_span(send_z, recv_z, sz_s, sz_r, d).wait_send()
        to_span(send_c, recv_c, sc_s, sc_r, d).wait_send()

    @pl.loop(1, groups)
    def _(d):
        to_group(d).wait_send()


def body(tiles, mems, field, vert, loc, alpha, xidx, yidx, members):
    slabs, cols, rows = field.shape
    own = cols // mems
    padded = -(-slabs // 16) * 16
    blocks = rows // LANES
    groups = tiles // SPAN
    dma = pltpu.SemaphoreType.DMA
    vmem = pltpu.VMEM
    result = pl.pallas_call(
        functools.partial(kernel, tiles, mems, slabs),
        out_shape=jax.ShapeDtypeStruct((own, padded, rows), BF16),
        in_specs=[pl.BlockSpec(memory_space=pl.ANY)] * 7,
        out_specs=pl.BlockSpec(memory_space=pltpu.VMEM),
        scratch_shapes=[
            vmem((slabs, cols, rows), BF16),
            vmem((slabs, cols, rows), BF16),
            vmem((blocks, padded * cols, LANES), F32),
            vmem((blocks, padded * cols, LANES), F32),
            vmem((mems, own, padded, rows), BF16),
            vmem((mems, own, padded, rows), BF16),
            vmem((own, padded, rows), BF16),
            vmem((blocks, padded, LANES), F32),
            vmem((blocks, padded, LANES), F32),
            vmem((blocks, padded, LANES), F32),
            vmem((SPAN, 16, LANES), BF16),
            vmem((SPAN, 16, LANES), BF16),
            vmem((SPAN, 16, LANES), BF16),
            vmem((mems, SPAN, 16, LANES), BF16),
            vmem((16, LANES), BF16),
            vmem((groups, 16, LANES), BF16),
            vmem((own, blocks * padded, LANES), F32),
            vmem((2, blocks, 2 * own, 16, LANES), F32),
            vmem((own, blocks * padded, LANES), BF16),
            vmem((2 * own, 2 * LANES, 3 * LANES), BF16),
            vmem((blocks * padded, 3 * LANES), F32),
            vmem((own, padded, rows), F32),
            vmem((own, padded, rows), F32),
            vmem((2 * own, 4, 8, LANES), F32),
            vmem((padded, padded), F32),
            vmem((padded, padded), F32),
            vmem(vert.shape, vert.dtype),
            vmem(loc.shape, loc.dtype),
            vmem(xidx.shape, xidx.dtype),
            pltpu.SMEM(alpha.shape, alpha.dtype),
            pltpu.SMEM(yidx.shape, yidx.dtype),
            dma((7,)),
            dma((mems,)),
            dma((mems,)),
            dma((SPAN,)),
            dma((SPAN,)),
            dma((SPAN,)),
            dma((SPAN,)),
            dma((groups,)),
            dma((groups,)),
            dma((mems,)),
            dma((mems,)),
        ],
        compiler_params=pltpu.CompilerParams(
            collective_id=0, has_side_effects=True, vmem_limit_bytes=60 * 2**20
        ),
    )(field, members, vert, loc, xidx, alpha, yidx)
    return jnp.swapaxes(result, 0, 1)[:slabs]


def solution(mesh):
    return jax.shard_map(
        functools.partial(body, mesh.shape["tile"], mesh.shape["mem"]),
        mesh=mesh,
        in_specs=(P(None, "tile", None), P(), P(), P(), P(), P(), P("mem", None, "tile", None)),
        out_specs=P(None, ("tile", "mem"), None),
        check_vma=False,
    )
```

```python
import functools

import jax
import jax.numpy as jnp
from jax import lax
from jax.experimental import pallas as pl
from jax.experimental.pallas import tpu as pltpu
from jax.sharding import PartitionSpec as P

MESH = pl.DeviceIdType.MESH
F32 = jnp.float32
BF16 = jnp.bfloat16
LANES = 128
SPAN = 16


def gains(a):
    return jnp.sqrt(1.0 - a * a), (1.0 - a * a) / jnp.sqrt(1.0 + a * a)


def extended(dst, matrix, pad, work):
    n = matrix.shape[-1]
    work[...] = jnp.zeros(work.shape, F32)
    work[0:n, 0:n] = matrix[0].astype(F32)
    i = lax.broadcasted_iota(jnp.int32, dst.shape, 0)
    j = lax.broadcasted_iota(jnp.int32, dst.shape, 1)
    keep = (i == j) & (i >= n) & (i < pad)
    dst[...] = jnp.where(keep, 1.0, work[...]).astype(BF16)


def kernel(
    tiles, mems, slabs,
    field, members, vert_hbm, loc_hbm, xidx_hbm, alpha_hbm, yidx_hbm,
    out,
    fbuf, mbuf, x32, m32, far_s, far_r, side_s, side_r, hold, ax, gfx, gbx,
    send_z, recv_z, send_c, entering_all, send_y, recv_y, base, reach,
    lines, weights, mixed, smooth, acc, tab, lmat, vmat, square_work, vert, loc, xidx, alpha, yidx,
    local_sem, sm_s, sm_r, sz_s, sz_r, sc_s, sc_r, sy_s, sy_r, sx_s, sx_r,
):
    tile = lax.axis_index("tile")
    mem = lax.axis_index("mem")
    groups = tiles // SPAN
    q = lax.rem(tile, SPAN)
    y = tile // SPAN
    cols = field.shape[1]
    rows = field.shape[2]
    blocks = rows // LANES
    own = cols // mems
    levels = vert.shape[-1]
    padded = x32.shape[1] // cols

    get_field = pltpu.make_async_copy(field, fbuf, local_sem.at[1])
    get_field.start()
    small = [
        pltpu.make_async_copy(src, dst, local_sem.at[2 + at])
        for at, (src, dst) in enumerate(
            (
                (xidx_hbm, xidx),
                (alpha_hbm, alpha),
                (yidx_hbm, yidx),
                (loc_hbm, loc),
                (vert_hbm, vert),
            )
        )
    ]
    for copy in small:
        copy.start()
    get_members = pltpu.make_async_copy(members.at[0], mbuf, local_sem.at[0])
    get_members.start()

    barrier = pltpu.get_barrier_semaphore()

    @pl.loop(1, mems)
    def _(d):
        pl.semaphore_signal(
            barrier, inc=1, device_id={"mem": lax.rem(mem + d, mems)}, device_id_type=MESH
        )

    @pl.loop(1, SPAN)
    def _(d):
        pl.semaphore_signal(
            barrier,
            inc=1,
            device_id={"tile": y * SPAN + lax.rem(q + d, SPAN)},
            device_id_type=MESH,
        )

    @pl.loop(1, groups)
    def _(d):
        pl.semaphore_signal(
            barrier,
            inc=1,
            device_id={"tile": lax.rem(y + d, groups) * SPAN + q},
            device_id_type=MESH,
        )

    for copy in small:
        copy.wait()
    sub = lax.broadcasted_iota(jnp.int32, (padded, LANES), 0)

    @pl.loop(0, blocks)
    def _(b):
        lane = pl.ds(pl.multiple_of(b * LANES, LANES), LANES)
        idx = xidx[:, lane]
        a = jnp.zeros(idx.shape, F32)
        for k in range(alpha.shape[0]):
            a = jnp.where(idx == k, alpha[k], a)
        wide = jnp.where(
            sub < levels,
            jnp.broadcast_to(a[0:1], (padded, LANES)),
            jnp.broadcast_to(a[1:2], (padded, LANES)),
        )
        fwd, back = gains(wide)
        ax[b] = wide
        gfx[b] = fwd
        gbx[b] = back

    def spread(src, dst):
        for b in range(blocks):
            dst[b, pl.ds(slabs * cols, (padded - slabs) * cols), :] = jnp.zeros(
                ((padded - slabs) * cols, LANES), F32
            )

        @pl.loop(0, slabs)
        def _(s):
            at = pl.ds(pl.multiple_of(s * cols, cols), cols)
            for b in range(blocks):
                dst[b, at, :] = src[s, :, b * LANES : (b + 1) * LANES].astype(F32)

    near = (lax.rem(mem + 1, mems), lax.rem(mem + mems - 1, mems))
    opposite = lax.rem(mem + 2, mems)
    halves = (slice(0, own // 2), slice(own // 2, own))

    def pass_far(side):
        return pltpu.make_async_remote_copy(
            src_ref=far_s.at[halves[side]],
            dst_ref=far_r.at[side],
            send_sem=sm_s.at[side],
            recv_sem=sm_r.at[side],
            device_id={"mem": near[side]},
            device_id_type=MESH,
        )

    def pass_near(side, half):
        return pltpu.make_async_remote_copy(
            src_ref=side_s.at[side, half],
            dst_ref=side_r.at[side, half],
            send_sem=sm_s.at[2 + 2 * side + half],
            recv_sem=sm_r.at[2 + 2 * side + half],
            device_id={"mem": near[side]},
            device_id_type=MESH,
        )

    wide_lanes = 2 * LANES
    half_own = own // 2

    def ensemble(peer, half, dst):
        @pl.loop(0, half_own)
        def _(k):
            col = peer * own + half * half_own + k
            for w in range(rows // wide_lanes):

                def column(src):
                    at = pl.ds(col, padded, stride=cols)
                    return jnp.concatenate([src[2 * w, at, :], src[2 * w + 1, at, :]], axis=1)

                m = column(m32)
                scaled = (m * column(x32)).astype(BF16)
                term = m * jnp.dot(lmat[...], scaled, preferred_element_type=F32)
                dst[k, :, w * wide_lanes : (w + 1) * wide_lanes] = term.astype(dst.dtype)

    quads = padded // 16

    def local_states(b, p):
        at = pl.ds(pl.multiple_of(p * 16, 16), 16)
        a, fwd, back = ax[b, at, :], gfx[b, at, :], gbx[b, at, :]
        f = jnp.zeros((16, LANES), F32)
        states = []
        for c in range(cols):
            f = a * f + fwd * x32[b, pl.ds(p * 16 * cols + c, 16, stride=cols), :]
            states.append(f)
        value = jnp.zeros((16, LANES), F32)
        backs = [None] * cols
        for c in reversed(range(cols)):
            value = a * value + back * states[c]
            backs[c] = value
        return states, backs

    def mine(values, k):
        value = values[k]
        for g in range(1, mems):
            value = jnp.where(mem == g, values[g * own + k], value)
        return value

    def to_span(src, dst, s_sem, r_sem, d):
        peer = lax.rem(q + d, SPAN)
        return pltpu.make_async_remote_copy(
            src_ref=src.at[peer],
            dst_ref=dst.at[q],
            send_sem=s_sem.at[peer],
            recv_sem=r_sem.at[q],
            device_id={"tile": y * SPAN + peer},
            device_id_type=MESH,
        )

    def from_span(src, dst, s_sem, r_sem, d):
        peer = lax.rem(q + d, SPAN)
        return pltpu.make_async_remote_copy(
            src_ref=src.at[peer],
            dst_ref=dst.at[peer],
            send_sem=s_sem.at[peer],
            recv_sem=r_sem.at[peer],
            device_id={"tile": y * SPAN + peer},
            device_id_type=MESH,
        )

    get_field.wait()
    spread(fbuf, x32)

    @pl.loop(0, blocks)
    def _(b):
        states, backs = local_states(b, mem)
        for h in range(2):
            part = slice(8 * h, 8 * h + 8)
            pair = jnp.concatenate([states[-1][part], backs[0][part]], axis=0)
            send_z[2 * b + h] = pair.astype(BF16)

    pl.semaphore_wait(barrier, (mems - 1) + (SPAN - 1) + (groups - 1))

    @pl.loop(1, SPAN)
    def _(d):
        to_span(send_z, recv_z, sz_s, sz_r, d).start()

    recv_z[q] = send_z[q]

    extended(lmat, loc, slabs, square_work)
    extended(vmat, vert, slabs, square_work)
    get_members.wait()
    spread(mbuf, m32)
    for half in range(2):
        ensemble(opposite, half, far_s.at[halves[half]])
        pass_far(half).start()
    for side in range(2):
        ensemble(near[side], 1 - side, side_s.at[side, 1 - side])
        pass_near(side, 1 - side).start()

    zero = jnp.zeros((8, LANES), F32)
    piece_at = pl.ds(pl.multiple_of(mem * 16 + lax.rem(q, 2) * 8, 8), 8)
    a = ax[q // 2, piece_at, :]
    back = gbx[q // 2, piece_at, :]
    f = jnp.ones_like(a)
    states = []
    for c in range(cols):
        f = a * f
        states.append(f)
    cross = zero
    for c in reversed(range(cols)):
        cross = a * cross + back * states[c]
    decay = states[-1]
    square = decay * decay
    total, fade, far_decay = zero, jnp.ones_like(a), jnp.ones_like(a)
    for _ in range(SPAN):
        total = total + fade
        fade = fade * square
        far_decay = far_decay * decay
    far_cross = cross * total

    @pl.loop(1, SPAN)
    def _(d):
        from_span(send_z, recv_z, sz_s, sz_r, d).wait_recv()

    def scan_span(f, b):
        enter_f, enter_b = [], [None] * SPAN
        pairs = [recv_z[i].astype(F32) for i in range(SPAN)]
        for i in range(SPAN):
            enter_f.append(f)
            f = pairs[i][0:8] + decay * f
        for i in reversed(range(SPAN)):
            enter_b[i] = b
            b = pairs[i][8:16] + cross * enter_f[i] + decay * b
        return f, b, enter_f, enter_b

    end, begin, _, _ = scan_span(zero, zero)
    send_y[...] = jnp.concatenate([end, begin], axis=0).astype(BF16)

    def to_group(d):
        peer = lax.rem(y + d, groups)
        return pltpu.make_async_remote_copy(
            src_ref=send_y,
            dst_ref=recv_y.at[y],
            send_sem=sy_s.at[peer],
            recv_sem=sy_r.at[y],
            device_id={"tile": peer * SPAN + q},
            device_id_type=MESH,
        )

    def from_group(d):
        peer = lax.rem(y + d, groups)
        return pltpu.make_async_remote_copy(
            src_ref=send_y,
            dst_ref=recv_y.at[peer],
            send_sem=sy_s.at[peer],
            recv_sem=sy_r.at[peer],
            device_id={"tile": peer * SPAN + q},
            device_id_type=MESH,
        )

    @pl.loop(1, groups)
    def _(d):
        to_group(d).start()

    recv_y[y] = send_y[...]

    @pl.loop(0, blocks)
    def _(b):
        @pl.loop(0, quads)
        def _(p):
            _, backs = local_states(b, p)
            at = pl.ds(pl.multiple_of(b * padded + p * 16, 16), 16)
            for k in range(own):
                base[k, at, :] = mine(backs, k)

        for kind in range(2):
            at = slice(0, 16) if kind == 0 else slice(padded - 16, padded)
            a, back = ax[b, at, :], gbx[b, at, :]
            f = jnp.ones((16, LANES), F32)
            states = []
            for c in range(cols):
                f = a * f
                states.append(f)
            value = jnp.zeros((16, LANES), F32)
            backs = [None] * cols
            for c in reversed(range(cols)):
                value = a * value + back * states[c]
                backs[c] = value
            for k in range(own):
                reach[kind, b, 2 * k] = mine(backs, k)
                reach[kind, b, 2 * k + 1] = mine(states[::-1], k)

    @pl.loop(1, groups)
    def _(d):
        from_group(d).wait_recv()

    pairs = [recv_y[i].astype(F32) for i in range(groups)]
    enter = []
    f = zero
    mine_f = zero
    for i in range(groups):
        enter.append(f)
        mine_f = jnp.where(y == i, f, mine_f)
        f = pairs[i][0:8] + far_decay * f
    b = zero
    mine_b = zero
    for i in reversed(range(groups)):
        mine_b = jnp.where(y == i, b, mine_b)
        b = pairs[i][8:16] + far_cross * enter[i] + far_decay * b
    _, _, enter_f, enter_b = scan_span(mine_f, mine_b)
    for i in range(SPAN):
        send_c[i] = jnp.concatenate([enter_f[i], enter_b[i]], axis=0).astype(BF16)

    recv_c = entering_all.at[mem]

    @pl.loop(1, SPAN)
    def _(d):
        to_span(send_c, recv_c, sc_s, sc_r, d).start()

    entering_all[mem, q] = send_c[q]

    for side in range(2):
        ensemble(near[side], side, hold.at[side])
    for side in range(2):
        pass_far(side).wait_recv()

        @pl.loop(0, half_own)
        def _(k):
            total = hold[side, k] + far_r[side, k].astype(F32)
            side_s[side, side, k] = total.astype(BF16)

        pass_near(side, side).start()

    for half in range(2):
        ensemble(mem, half, acc.at[halves[half]])

    @pl.loop(1, SPAN)
    def _(d):
        from_span(send_c, recv_c, sc_s, sc_r, d).wait_recv()

    def gather(d):
        return pltpu.make_async_remote_copy(
            src_ref=entering_all.at[mem],
            dst_ref=entering_all.at[mem],
            send_sem=sx_s.at[d],
            recv_sem=sx_r.at[d],
            device_id={"mem": lax.rem(mem + d, mems)},
            device_id_type=MESH,
        )

    def gathered(d):
        peer = lax.rem(mem + mems - d, mems)
        return pltpu.make_async_remote_copy(
            src_ref=entering_all.at[peer],
            dst_ref=entering_all.at[peer],
            send_sem=sx_s.at[d],
            recv_sem=sx_r.at[d],
            device_id={"mem": lax.rem(mem + d, mems)},
            device_id_type=MESH,
        )

    for d in (2, 1, 3):
        gather(d).start()

    lane8 = lax.broadcasted_iota(jnp.int32, (8, LANES), 1)
    sub8 = lax.broadcasted_iota(jnp.int32, (8, LANES), 0)
    row_i = lax.broadcasted_iota(jnp.int32, (LANES, LANES), 0)
    row_j = lax.broadcasted_iota(jnp.int32, (LANES, LANES), 1)

    def geometric(count, ratio):
        value = jnp.zeros(count.shape, F32)
        reached = jnp.ones(count.shape, F32)
        part = jnp.float32(1.0)
        for bit in range(8):
            has = (count & (1 << bit)) != 0
            value = jnp.where(has, value + reached * part, value)
            reached = jnp.where(has, reached * ratio, reached)
            part = part * (1.0 + ratio)
            ratio = ratio * ratio
        return value

    @pl.loop(0, own)
    def _(c):
        col = tile * cols + mem * own + c
        tables = []
        for kind in range(2):
            coeff = alpha[yidx[kind, col]]
            a = jnp.full((8, LANES), coeff, F32)
            fwd, back = gains(a)
            rate = jnp.log(jnp.maximum(a, 1e-37))

            def tall(x):
                return jnp.broadcast_to(x[0:1], (LANES, LANES))

            def power(exponent, log_a):
                return jnp.exp(exponent.astype(F32) * log_a)

            ratio = coeff * coeff
            inner = power(jnp.abs(row_i - row_j), tall(rate)) * tall(fwd * back)
            inner = inner * geometric(LANES - jnp.maximum(row_i, row_j), ratio)
            ends = power(LANES - 1 - row_i, tall(rate)) * tall(fwd)
            starts = jnp.broadcast_to(inner[:, 0:1], (LANES, LANES))
            for at, part in enumerate((inner, ends, starts)):
                high = part.astype(BF16)
                low = (part - high.astype(F32)).astype(BF16)
                lane = slice(at * LANES, (at + 1) * LANES)
                weights[2 * c + kind, 0:LANES, lane] = high
                weights[2 * c + kind, LANES : 2 * LANES, lane] = low
            far = coeff
            for _ in range(7):
                far = far * far
            whole = geometric(jnp.full((8, LANES), LANES, jnp.int32), ratio)
            tables.append(
                (
                    back * power(lane8 + 1, rate) * geometric(LANES - lane8, ratio),
                    power(LANES - lane8, rate),
                    jnp.full((8, LANES), far, F32),
                    back * a * whole,
                )
            )
        for at, (first, second) in enumerate(zip(*tables)):
            tab[2 * c, at] = first
            tab[2 * c + 1, at] = jnp.where(sub8 < levels % 8, first, second)

    def add_carries(p):
        kind = p // (quads - 1)
        for b in range(blocks):
            low = entering_all[p, 2 * b].astype(F32)
            high = entering_all[p, 2 * b + 1].astype(F32)
            f = jnp.concatenate([low[0:8], high[0:8]], axis=0)
            bk = jnp.concatenate([low[8:16], high[8:16]], axis=0)
            at = pl.ds(pl.multiple_of(b * padded + p * 16, 16), 16)
            for k in range(own):
                value = base[k, at, :] + reach[kind, b, 2 * k] * f + reach[kind, b, 2 * k + 1] * bk
                lines[k, at, :] = value.astype(BF16)

    add_carries(mem)
    for d in (1, 3, 2):
        gathered(d).wait_recv()
        add_carries(lax.rem(mem + mems - d, mems))

    last = padded - 8

    @pl.loop(0, own)
    def _(c):
        x = jnp.concatenate([lines[c], lines[c]], axis=1)
        mixed[...] = jnp.dot(x, weights[2 * c], preferred_element_type=F32)
        tail = jnp.concatenate(
            [lines[c, (b + 1) * padded - 16 : (b + 1) * padded, :] for b in range(blocks)], axis=0
        )
        tail = jnp.concatenate([tail, tail], axis=1)
        other = jnp.dot(tail, weights[2 * c + 1], preferred_element_type=F32)
        pick = jnp.concatenate([sub8] * 3, axis=1) < levels % 8
        for b in range(blocks):
            at = slice(b * padded + last, (b + 1) * padded)
            mixed[at, :] = jnp.where(pick, mixed[at, :], other[16 * b + 8 : 16 * b + 16])

        for g in range(padded // 8):
            t = 2 * c + g // (levels // 8)
            from_left, from_right, far, cross = tab[t, 0], tab[t, 1], tab[t, 2], tab[t, 3]

            def block(b, part):
                at = slice(b * padded + g * 8, b * padded + g * 8 + 8)
                return mixed[at, part * LANES : (part + 1) * LANES]

            state = jnp.zeros((8, LANES), F32)
            entering = []
            for b in range(blocks):
                entering.append(state)
                state = block(b, 1) + far * state
            state = jnp.zeros((8, LANES), F32)
            for b in reversed(range(blocks)):
                value = block(b, 0) + from_left * entering[b] + from_right * state
                smooth[c, g * 8 : g * 8 + 8, b * LANES : (b + 1) * LANES] = value
                state = block(b, 2) + cross * entering[b] + far * state

    for side in range(2):
        for half in range(2):
            pass_near(side, half).wait_recv()

    for half in range(2):

        @pl.loop(0, half_own)
        def _(k):
            c = half * half_own + k
            for w in range(rows // wide_lanes):
                lane = slice(w * wide_lanes, (w + 1) * wide_lanes)
                others = side_r[0, half, k, :, lane].astype(F32)
                others = others + side_r[1, half, k, :, lane].astype(F32)
                x = smooth[c, :, lane].astype(BF16)
                static = jnp.dot(vmat[...], x, preferred_element_type=F32)
                out[c, :, lane] = (static + (acc[c, :, lane] + others) / (mems - 1)).astype(BF16)

    for d in (1, 2, 3):
        gather(d).wait_send()
    for side in range(2):
        pass_far(side).wait_send()
        for half in range(2):
            pass_near(side, half).wait_send()

    @pl.loop(1, SPAN)
    def _(d):
        to_span(send_z, recv_z, sz_s, sz_r, d).wait_send()
        to_span(send_c, recv_c, sc_s, sc_r, d).wait_send()

    @pl.loop(1, groups)
    def _(d):
        to_group(d).wait_send()


def body(tiles, mems, field, vert, loc, alpha, xidx, yidx, members):
    slabs, cols, rows = field.shape
    own = cols // mems
    padded = -(-slabs // 16) * 16
    blocks = rows // LANES
    groups = tiles // SPAN
    dma = pltpu.SemaphoreType.DMA
    vmem = pltpu.VMEM
    result = pl.pallas_call(
        functools.partial(kernel, tiles, mems, slabs),
        out_shape=jax.ShapeDtypeStruct((own, padded, rows), BF16),
        in_specs=[pl.BlockSpec(memory_space=pl.ANY)] * 7,
        out_specs=pl.BlockSpec(memory_space=pltpu.VMEM),
        scratch_shapes=[
            vmem((slabs, cols, rows), BF16),
            vmem((slabs, cols, rows), BF16),
            vmem((blocks, padded * cols, LANES), F32),
            vmem((blocks, padded * cols, LANES), F32),
            vmem((own, padded, rows), BF16),
            vmem((2, own // 2, padded, rows), BF16),
            vmem((2, 2, own // 2, padded, rows), BF16),
            vmem((2, 2, own // 2, padded, rows), BF16),
            vmem((2, own // 2, padded, rows), F32),
            vmem((blocks, padded, LANES), F32),
            vmem((blocks, padded, LANES), F32),
            vmem((blocks, padded, LANES), F32),
            vmem((SPAN, 16, LANES), BF16),
            vmem((SPAN, 16, LANES), BF16),
            vmem((SPAN, 16, LANES), BF16),
            vmem((mems, SPAN, 16, LANES), BF16),
            vmem((16, LANES), BF16),
            vmem((groups, 16, LANES), BF16),
            vmem((own, blocks * padded, LANES), F32),
            vmem((2, blocks, 2 * own, 16, LANES), F32),
            vmem((own, blocks * padded, LANES), BF16),
            vmem((2 * own, 2 * LANES, 3 * LANES), BF16),
            vmem((blocks * padded, 3 * LANES), F32),
            vmem((own, padded, rows), F32),
            vmem((own, padded, rows), F32),
            vmem((2 * own, 4, 8, LANES), F32),
            vmem((padded, padded), BF16),
            vmem((padded, padded), BF16),
            vmem((padded, padded), F32),
            vmem(vert.shape, vert.dtype),
            vmem(loc.shape, loc.dtype),
            vmem(xidx.shape, xidx.dtype),
            pltpu.SMEM(alpha.shape, alpha.dtype),
            pltpu.SMEM(yidx.shape, yidx.dtype),
            dma((7,)),
            dma((6,)),
            dma((6,)),
            dma((SPAN,)),
            dma((SPAN,)),
            dma((SPAN,)),
            dma((SPAN,)),
            dma((groups,)),
            dma((groups,)),
            dma((mems,)),
            dma((mems,)),
        ],
        compiler_params=pltpu.CompilerParams(
            collective_id=0, has_side_effects=True, vmem_limit_bytes=60 * 2**20
        ),
    )(field, members, vert, loc, xidx, alpha, yidx)
    return jnp.swapaxes(result, 0, 1)[:slabs]


def solution(mesh):
    return jax.shard_map(
        functools.partial(body, mesh.shape["tile"], mesh.shape["mem"]),
        mesh=mesh,
        in_specs=(P(None, "tile", None), P(), P(), P(), P(), P(), P("mem", None, "tile", None)),
        out_specs=P(None, ("tile", "mem"), None),
        check_vma=False,
    )
```

```python
import functools

import jax
import jax.numpy as jnp
from jax import lax
from jax.experimental import pallas as pl
from jax.experimental.pallas import tpu as pltpu
from jax.sharding import PartitionSpec as P

MESH = pl.DeviceIdType.MESH
F32 = jnp.float32
BF16 = jnp.bfloat16
LANES = 128
SPAN = 16


def gains(a):
    return jnp.sqrt(1.0 - a * a), (1.0 - a * a) / jnp.sqrt(1.0 + a * a)


def extended(dst, matrix, pad, work):
    n = matrix.shape[-1]
    work[...] = jnp.zeros(work.shape, F32)
    work[0:n, 0:n] = matrix[0].astype(F32)
    i = lax.broadcasted_iota(jnp.int32, dst.shape, 0)
    j = lax.broadcasted_iota(jnp.int32, dst.shape, 1)
    keep = (i == j) & (i >= n) & (i < pad)
    dst[...] = jnp.where(keep, 1.0, work[...]).astype(BF16)


def kernel(
    tiles, mems, slabs,
    field, members, vert_hbm, loc_hbm, xidx_hbm, alpha_hbm, yidx_hbm,
    out,
    fbuf, mbuf, x32, m32, far_s, far_r, side_s, side_r, hold, ax, gfx, gbx,
    send_z, recv_z, send_c, entering_all, send_y, recv_y, base, reach,
    lines, weights, mixed, smooth, acc, tab, lmat, vmat, square_work, vert, loc, xidx, alpha, yidx,
    local_sem, sm_s, sm_r, sz_s, sz_r, sc_s, sc_r, sy_s, sy_r, sx_s, sx_r,
):
    tile = lax.axis_index("tile")
    mem = lax.axis_index("mem")
    groups = tiles // SPAN
    q = lax.rem(tile, SPAN)
    y = tile // SPAN
    cols = field.shape[1]
    rows = field.shape[2]
    blocks = rows // LANES
    own = cols // mems
    levels = vert.shape[-1]
    padded = -(-slabs // 16) * 16
    pitch = x32.shape[1] // padded

    get_field = pltpu.make_async_copy(field, fbuf, local_sem.at[1])
    get_field.start()
    small = [
        pltpu.make_async_copy(src, dst, local_sem.at[2 + at])
        for at, (src, dst) in enumerate(
            (
                (xidx_hbm, xidx),
                (alpha_hbm, alpha),
                (yidx_hbm, yidx),
                (loc_hbm, loc),
                (vert_hbm, vert),
            )
        )
    ]
    for copy in small:
        copy.start()
    get_members = pltpu.make_async_copy(members.at[0], mbuf, local_sem.at[0])
    get_members.start()

    barrier = pltpu.get_barrier_semaphore()

    @pl.loop(1, mems)
    def _(d):
        pl.semaphore_signal(
            barrier, inc=1, device_id={"mem": lax.rem(mem + d, mems)}, device_id_type=MESH
        )

    @pl.loop(1, SPAN)
    def _(d):
        pl.semaphore_signal(
            barrier,
            inc=1,
            device_id={"tile": y * SPAN + lax.rem(q + d, SPAN)},
            device_id_type=MESH,
        )

    @pl.loop(1, groups)
    def _(d):
        pl.semaphore_signal(
            barrier,
            inc=1,
            device_id={"tile": lax.rem(y + d, groups) * SPAN + q},
            device_id_type=MESH,
        )

    for copy in small:
        copy.wait()
    sub = lax.broadcasted_iota(jnp.int32, (padded, LANES), 0)

    @pl.loop(0, blocks)
    def _(b):
        lane = pl.ds(pl.multiple_of(b * LANES, LANES), LANES)
        idx = xidx[:, lane]
        a = jnp.zeros(idx.shape, F32)
        for k in range(alpha.shape[0]):
            a = jnp.where(idx == k, alpha[k], a)
        wide = jnp.where(
            sub < levels,
            jnp.broadcast_to(a[0:1], (padded, LANES)),
            jnp.broadcast_to(a[1:2], (padded, LANES)),
        )
        fwd, back = gains(wide)
        ax[b] = wide
        gfx[b] = fwd
        gbx[b] = back

    def spread(src, dst):
        def put(view, s, i):
            for b in range(blocks):
                part = src[s, :, b * LANES : (b + 1) * LANES].astype(F32)
                view[b, i * pitch : i * pitch + cols, :] = part

        done = slabs // 8 * 8

        @pl.loop(0, slabs // 8)
        def _(g):
            at = pl.ds(pl.multiple_of(g * 8 * pitch, 8), 8 * pitch)
            view = dst.at[:, at, :]
            for i in range(8):
                put(view, 8 * g + i, i)

        for s in range(done, slabs):
            put(dst.at[:, done * pitch : padded * pitch, :], s, s - done)
        for b in range(blocks):
            left = slice(slabs * pitch, padded * pitch)
            dst[b, left, :] = jnp.zeros(((padded - slabs) * pitch, LANES), F32)

    near = (lax.rem(mem + 1, mems), lax.rem(mem + mems - 1, mems))
    opposite = lax.rem(mem + 2, mems)
    halves = (slice(0, own // 2), slice(own // 2, own))

    def pass_far(side):
        return pltpu.make_async_remote_copy(
            src_ref=far_s.at[halves[side]],
            dst_ref=far_r.at[side],
            send_sem=sm_s.at[side],
            recv_sem=sm_r.at[side],
            device_id={"mem": near[side]},
            device_id_type=MESH,
        )

    def pass_near(side, half):
        return pltpu.make_async_remote_copy(
            src_ref=side_s.at[side, half],
            dst_ref=side_r.at[side, half],
            send_sem=sm_s.at[2 + 2 * side + half],
            recv_sem=sm_r.at[2 + 2 * side + half],
            device_id={"mem": near[side]},
            device_id_type=MESH,
        )

    wide_lanes = 2 * LANES
    half_own = own // 2

    def ensemble(peer, half, dst):
        @pl.loop(0, half_own)
        def _(k):
            col = peer * own + half * half_own + k
            for w in range(rows // wide_lanes):

                def column(src):
                    at = pl.ds(col, padded, stride=pitch)
                    return jnp.concatenate([src[2 * w, at, :], src[2 * w + 1, at, :]], axis=1)

                m = column(m32)
                scaled = (m * column(x32)).astype(BF16)
                term = m * jnp.dot(lmat[...], scaled, preferred_element_type=F32)
                dst[k, :, w * wide_lanes : (w + 1) * wide_lanes] = term.astype(dst.dtype)

    quads = padded // 16

    def local_states(b, p):
        at = pl.ds(pl.multiple_of(p * 16, 16), 16)
        a, fwd, back = ax[b, at, :], gfx[b, at, :], gbx[b, at, :]
        f = jnp.zeros((16, LANES), F32)
        states = []
        for c in range(cols):
            f = a * f + fwd * x32[b, pl.ds(p * 16 * pitch + c, 16, stride=pitch), :]
            states.append(f)
        value = jnp.zeros((16, LANES), F32)
        backs = [None] * cols
        for c in reversed(range(cols)):
            value = a * value + back * states[c]
            backs[c] = value
        return states, backs

    def mine(values, k):
        value = values[k]
        for g in range(1, mems):
            value = jnp.where(mem == g, values[g * own + k], value)
        return value

    def to_span(src, dst, s_sem, r_sem, d):
        peer = lax.rem(q + d, SPAN)
        return pltpu.make_async_remote_copy(
            src_ref=src.at[peer],
            dst_ref=dst.at[q],
            send_sem=s_sem.at[peer],
            recv_sem=r_sem.at[q],
            device_id={"tile": y * SPAN + peer},
            device_id_type=MESH,
        )

    def from_span(src, dst, s_sem, r_sem, d):
        peer = lax.rem(q + d, SPAN)
        return pltpu.make_async_remote_copy(
            src_ref=src.at[peer],
            dst_ref=dst.at[peer],
            send_sem=s_sem.at[peer],
            recv_sem=r_sem.at[peer],
            device_id={"tile": y * SPAN + peer},
            device_id_type=MESH,
        )

    get_field.wait()
    spread(fbuf, x32)

    @pl.loop(0, blocks)
    def _(b):
        states, backs = local_states(b, mem)
        for h in range(2):
            part = slice(8 * h, 8 * h + 8)
            pair = jnp.concatenate([states[-1][part], backs[0][part]], axis=0)
            send_z[2 * b + h] = pair.astype(BF16)

    pl.semaphore_wait(barrier, (mems - 1) + (SPAN - 1) + (groups - 1))

    @pl.loop(1, SPAN)
    def _(d):
        to_span(send_z, recv_z, sz_s, sz_r, d).start()

    recv_z[q] = send_z[q]

    extended(lmat, loc, slabs, square_work)
    extended(vmat, vert, slabs, square_work)
    get_members.wait()
    spread(mbuf, m32)
    for half in range(2):
        ensemble(opposite, half, far_s.at[halves[half]])
        pass_far(half).start()
    for side in range(2):
        ensemble(near[side], 1 - side, side_s.at[side, 1 - side])
        pass_near(side, 1 - side).start()

    zero = jnp.zeros((8, LANES), F32)
    piece_at = pl.ds(pl.multiple_of(mem * 16 + lax.rem(q, 2) * 8, 8), 8)
    a = ax[q // 2, piece_at, :]
    back = gbx[q // 2, piece_at, :]
    f = jnp.ones_like(a)
    states = []
    for c in range(cols):
        f = a * f
        states.append(f)
    cross = zero
    for c in reversed(range(cols)):
        cross = a * cross + back * states[c]
    decay = states[-1]
    square = decay * decay
    total, fade, far_decay = zero, jnp.ones_like(a), jnp.ones_like(a)
    for _ in range(SPAN):
        total = total + fade
        fade = fade * square
        far_decay = far_decay * decay
    far_cross = cross * total

    @pl.loop(1, SPAN)
    def _(d):
        from_span(send_z, recv_z, sz_s, sz_r, d).wait_recv()

    def scan_span(f, b):
        enter_f, enter_b = [], [None] * SPAN
        pairs = [recv_z[i].astype(F32) for i in range(SPAN)]
        for i in range(SPAN):
            enter_f.append(f)
            f = pairs[i][0:8] + decay * f
        for i in reversed(range(SPAN)):
            enter_b[i] = b
            b = pairs[i][8:16] + cross * enter_f[i] + decay * b
        return f, b, enter_f, enter_b

    end, begin, _, _ = scan_span(zero, zero)
    send_y[...] = jnp.concatenate([end, begin], axis=0).astype(BF16)

    def to_group(d):
        peer = lax.rem(y + d, groups)
        return pltpu.make_async_remote_copy(
            src_ref=send_y,
            dst_ref=recv_y.at[y],
            send_sem=sy_s.at[peer],
            recv_sem=sy_r.at[y],
            device_id={"tile": peer * SPAN + q},
            device_id_type=MESH,
        )

    def from_group(d):
        peer = lax.rem(y + d, groups)
        return pltpu.make_async_remote_copy(
            src_ref=send_y,
            dst_ref=recv_y.at[peer],
            send_sem=sy_s.at[peer],
            recv_sem=sy_r.at[peer],
            device_id={"tile": peer * SPAN + q},
            device_id_type=MESH,
        )

    @pl.loop(1, groups)
    def _(d):
        to_group(d).start()

    recv_y[y] = send_y[...]

    @pl.loop(0, blocks)
    def _(b):
        @pl.loop(0, quads)
        def _(p):
            _, backs = local_states(b, p)
            at = pl.ds(pl.multiple_of(b * padded + p * 16, 16), 16)
            for k in range(own):
                base[k, at, :] = mine(backs, k)

        for kind in range(2):
            at = slice(0, 16) if kind == 0 else slice(padded - 16, padded)
            a, back = ax[b, at, :], gbx[b, at, :]
            f = jnp.ones((16, LANES), F32)
            states = []
            for c in range(cols):
                f = a * f
                states.append(f)
            value = jnp.zeros((16, LANES), F32)
            backs = [None] * cols
            for c in reversed(range(cols)):
                value = a * value + back * states[c]
                backs[c] = value
            for k in range(own):
                reach[kind, b, 2 * k] = mine(backs, k)
                reach[kind, b, 2 * k + 1] = mine(states[::-1], k)

    @pl.loop(1, groups)
    def _(d):
        from_group(d).wait_recv()

    pairs = [recv_y[i].astype(F32) for i in range(groups)]
    enter = []
    f = zero
    mine_f = zero
    for i in range(groups):
        enter.append(f)
        mine_f = jnp.where(y == i, f, mine_f)
        f = pairs[i][0:8] + far_decay * f
    b = zero
    mine_b = zero
    for i in reversed(range(groups)):
        mine_b = jnp.where(y == i, b, mine_b)
        b = pairs[i][8:16] + far_cross * enter[i] + far_decay * b
    _, _, enter_f, enter_b = scan_span(mine_f, mine_b)
    for i in range(SPAN):
        send_c[i] = jnp.concatenate([enter_f[i], enter_b[i]], axis=0).astype(BF16)

    recv_c = entering_all.at[mem]

    @pl.loop(1, SPAN)
    def _(d):
        to_span(send_c, recv_c, sc_s, sc_r, d).start()

    entering_all[mem, q] = send_c[q]

    for side in range(2):
        ensemble(near[side], side, hold.at[side])
    for side in range(2):
        pass_far(side).wait_recv()

        @pl.loop(0, half_own)
        def _(k):
            total = hold[side, k] + far_r[side, k].astype(F32)
            side_s[side, side, k] = total.astype(BF16)

        pass_near(side, side).start()

    for half in range(2):
        ensemble(mem, half, acc.at[halves[half]])

    @pl.loop(1, SPAN)
    def _(d):
        from_span(send_c, recv_c, sc_s, sc_r, d).wait_recv()

    def gather(d):
        return pltpu.make_async_remote_copy(
            src_ref=entering_all.at[mem],
            dst_ref=entering_all.at[mem],
            send_sem=sx_s.at[d],
            recv_sem=sx_r.at[d],
            device_id={"mem": lax.rem(mem + d, mems)},
            device_id_type=MESH,
        )

    def gathered(d):
        peer = lax.rem(mem + mems - d, mems)
        return pltpu.make_async_remote_copy(
            src_ref=entering_all.at[peer],
            dst_ref=entering_all.at[peer],
            send_sem=sx_s.at[d],
            recv_sem=sx_r.at[d],
            device_id={"mem": lax.rem(mem + d, mems)},
            device_id_type=MESH,
        )

    for d in (2, 1, 3):
        gather(d).start()

    lane8 = lax.broadcasted_iota(jnp.int32, (8, LANES), 1)
    sub8 = lax.broadcasted_iota(jnp.int32, (8, LANES), 0)
    row_i = lax.broadcasted_iota(jnp.int32, (LANES, LANES), 0)
    row_j = lax.broadcasted_iota(jnp.int32, (LANES, LANES), 1)

    def geometric(count, ratio):
        value = jnp.zeros(count.shape, F32)
        reached = jnp.ones(count.shape, F32)
        part = jnp.float32(1.0)
        for bit in range(8):
            has = (count & (1 << bit)) != 0
            value = jnp.where(has, value + reached * part, value)
            reached = jnp.where(has, reached * ratio, reached)
            part = part * (1.0 + ratio)
            ratio = ratio * ratio
        return value

    @pl.loop(0, own)
    def _(c):
        col = tile * cols + mem * own + c
        tables = []
        for kind in range(2):
            coeff = alpha[yidx[kind, col]]
            a = jnp.full((8, LANES), coeff, F32)
            fwd, back = gains(a)
            rate = jnp.log(jnp.maximum(a, 1e-37))

            def tall(x):
                return jnp.broadcast_to(x[0:1], (LANES, LANES))

            def power(exponent, log_a):
                return jnp.exp(exponent.astype(F32) * log_a)

            ratio = coeff * coeff
            inner = power(jnp.abs(row_i - row_j), tall(rate)) * tall(fwd * back)
            inner = inner * geometric(LANES - jnp.maximum(row_i, row_j), ratio)
            ends = power(LANES - 1 - row_i, tall(rate)) * tall(fwd)
            starts = jnp.broadcast_to(inner[:, 0:1], (LANES, LANES))
            for at, part in enumerate((inner, ends, starts)):
                high = part.astype(BF16)
                low = (part - high.astype(F32)).astype(BF16)
                lane = slice(at * LANES, (at + 1) * LANES)
                weights[2 * c + kind, 0:LANES, lane] = high
                weights[2 * c + kind, LANES : 2 * LANES, lane] = low
            far = coeff
            for _ in range(7):
                far = far * far
            whole = geometric(jnp.full((8, LANES), LANES, jnp.int32), ratio)
            tables.append(
                (
                    back * power(lane8 + 1, rate) * geometric(LANES - lane8, ratio),
                    power(LANES - lane8, rate),
                    jnp.full((8, LANES), far, F32),
                    back * a * whole,
                )
            )
        for at, (first, second) in enumerate(zip(*tables)):
            tab[2 * c, at] = first
            tab[2 * c + 1, at] = jnp.where(sub8 < levels % 8, first, second)

    def add_carries(p):
        kind = p // (quads - 1)
        for b in range(blocks):
            low = entering_all[p, 2 * b].astype(F32)
            high = entering_all[p, 2 * b + 1].astype(F32)
            f = jnp.concatenate([low[0:8], high[0:8]], axis=0)
            bk = jnp.concatenate([low[8:16], high[8:16]], axis=0)
            at = pl.ds(pl.multiple_of(b * padded + p * 16, 16), 16)
            for k in range(own):
                value = base[k, at, :] + reach[kind, b, 2 * k] * f + reach[kind, b, 2 * k + 1] * bk
                lines[k, at, :] = value.astype(BF16)

    add_carries(mem)
    for d in (1, 3, 2):
        gathered(d).wait_recv()
        add_carries(lax.rem(mem + mems - d, mems))

    last = padded - 8

    @pl.loop(0, own)
    def _(c):
        x = jnp.concatenate([lines[c], lines[c]], axis=1)
        mixed[...] = jnp.dot(x, weights[2 * c], preferred_element_type=F32)
        tail = jnp.concatenate(
            [lines[c, (b + 1) * padded - 16 : (b + 1) * padded, :] for b in range(blocks)], axis=0
        )
        tail = jnp.concatenate([tail, tail], axis=1)
        other = jnp.dot(tail, weights[2 * c + 1], preferred_element_type=F32)
        pick = jnp.concatenate([sub8] * 3, axis=1) < levels % 8
        for b in range(blocks):
            at = slice(b * padded + last, (b + 1) * padded)
            mixed[at, :] = jnp.where(pick, mixed[at, :], other[16 * b + 8 : 16 * b + 16])

        for g in range(padded // 8):
            t = 2 * c + g // (levels // 8)
            from_left, from_right, far, cross = tab[t, 0], tab[t, 1], tab[t, 2], tab[t, 3]

            def block(b, part):
                at = slice(b * padded + g * 8, b * padded + g * 8 + 8)
                return mixed[at, part * LANES : (part + 1) * LANES]

            state = jnp.zeros((8, LANES), F32)
            entering = []
            for b in range(blocks):
                entering.append(state)
                state = block(b, 1) + far * state
            state = jnp.zeros((8, LANES), F32)
            for b in reversed(range(blocks)):
                value = block(b, 0) + from_left * entering[b] + from_right * state
                smooth[c, g * 8 : g * 8 + 8, b * LANES : (b + 1) * LANES] = value
                state = block(b, 2) + cross * entering[b] + far * state

    for side in range(2):
        for half in range(2):
            pass_near(side, half).wait_recv()

    for half in range(2):

        @pl.loop(0, half_own)
        def _(k):
            c = half * half_own + k
            for w in range(rows // wide_lanes):
                lane = slice(w * wide_lanes, (w + 1) * wide_lanes)
                others = side_r[0, half, k, :, lane].astype(F32)
                others = others + side_r[1, half, k, :, lane].astype(F32)
                x = smooth[c, :, lane].astype(BF16)
                static = jnp.dot(vmat[...], x, preferred_element_type=F32)
                out[c, :, lane] = (static + (acc[c, :, lane] + others) / (mems - 1)).astype(BF16)

    for d in (1, 2, 3):
        gather(d).wait_send()
    for side in range(2):
        pass_far(side).wait_send()
        for half in range(2):
            pass_near(side, half).wait_send()

    @pl.loop(1, SPAN)
    def _(d):
        to_span(send_z, recv_z, sz_s, sz_r, d).wait_send()
        to_span(send_c, recv_c, sc_s, sc_r, d).wait_send()

    @pl.loop(1, groups)
    def _(d):
        to_group(d).wait_send()


def body(tiles, mems, field, vert, loc, alpha, xidx, yidx, members):
    slabs, cols, rows = field.shape
    own = cols // mems
    padded = -(-slabs // 16) * 16
    blocks = rows // LANES
    groups = tiles // SPAN
    dma = pltpu.SemaphoreType.DMA
    vmem = pltpu.VMEM
    result = pl.pallas_call(
        functools.partial(kernel, tiles, mems, slabs),
        out_shape=jax.ShapeDtypeStruct((own, padded, rows), BF16),
        in_specs=[pl.BlockSpec(memory_space=pl.ANY)] * 7,
        out_specs=pl.BlockSpec(memory_space=pltpu.VMEM),
        scratch_shapes=[
            vmem((slabs, cols, rows), BF16),
            vmem((slabs, cols, rows), BF16),
            vmem((blocks, padded * (cols + 1), LANES), F32),
            vmem((blocks, padded * (cols + 1), LANES), F32),
            vmem((own, padded, rows), BF16),
            vmem((2, own // 2, padded, rows), BF16),
            vmem((2, 2, own // 2, padded, rows), BF16),
            vmem((2, 2, own // 2, padded, rows), BF16),
            vmem((2, own // 2, padded, rows), F32),
            vmem((blocks, padded, LANES), F32),
            vmem((blocks, padded, LANES), F32),
            vmem((blocks, padded, LANES), F32),
            vmem((SPAN, 16, LANES), BF16),
            vmem((SPAN, 16, LANES), BF16),
            vmem((SPAN, 16, LANES), BF16),
            vmem((mems, SPAN, 16, LANES), BF16),
            vmem((16, LANES), BF16),
            vmem((groups, 16, LANES), BF16),
            vmem((own, blocks * padded, LANES), F32),
            vmem((2, blocks, 2 * own, 16, LANES), F32),
            vmem((own, blocks * padded, LANES), BF16),
            vmem((2 * own, 2 * LANES, 3 * LANES), BF16),
            vmem((blocks * padded, 3 * LANES), F32),
            vmem((own, padded, rows), F32),
            vmem((own, padded, rows), F32),
            vmem((2 * own, 4, 8, LANES), F32),
            vmem((padded, padded), BF16),
            vmem((padded, padded), BF16),
            vmem((padded, padded), F32),
            vmem(vert.shape, vert.dtype),
            vmem(loc.shape, loc.dtype),
            vmem(xidx.shape, xidx.dtype),
            pltpu.SMEM(alpha.shape, alpha.dtype),
            pltpu.SMEM(yidx.shape, yidx.dtype),
            dma((7,)),
            dma((6,)),
            dma((6,)),
            dma((SPAN,)),
            dma((SPAN,)),
            dma((SPAN,)),
            dma((SPAN,)),
            dma((groups,)),
            dma((groups,)),
            dma((mems,)),
            dma((mems,)),
        ],
        compiler_params=pltpu.CompilerParams(
            collective_id=0, has_side_effects=True, vmem_limit_bytes=60 * 2**20
        ),
    )(field, members, vert, loc, xidx, alpha, yidx)
    return jnp.swapaxes(result, 0, 1)[:slabs]


def solution(mesh):
    return jax.shard_map(
        functools.partial(body, mesh.shape["tile"], mesh.shape["mem"]),
        mesh=mesh,
        in_specs=(P(None, "tile", None), P(), P(), P(), P(), P(), P("mem", None, "tile", None)),
        out_specs=P(None, ("tile", "mem"), None),
        check_vma=False,
    )
```

```python
import functools

import jax
import jax.numpy as jnp
from jax import lax
from jax.experimental import pallas as pl
from jax.experimental.pallas import tpu as pltpu
from jax.sharding import PartitionSpec as P

MESH = pl.DeviceIdType.MESH
F32 = jnp.float32
BF16 = jnp.bfloat16
LANES = 128
SPAN = 16


def far_first(size):
    return sorted(range(1, size), key=lambda d: abs(2 * d - size))


def gains(a):
    return jnp.sqrt(1.0 - a * a), (1.0 - a * a) / jnp.sqrt(1.0 + a * a)


def extended(dst, matrix, pad, work):
    n = matrix.shape[-1]
    work[...] = jnp.zeros(work.shape, F32)
    work[0:n, 0:n] = matrix[0].astype(F32)
    i = lax.broadcasted_iota(jnp.int32, dst.shape, 0)
    j = lax.broadcasted_iota(jnp.int32, dst.shape, 1)
    keep = (i == j) & (i >= n) & (i < pad)
    dst[...] = jnp.where(keep, 1.0, work[...]).astype(BF16)


def kernel(
    tiles, mems, slabs,
    field, members, vert_hbm, loc_hbm, xidx_hbm, alpha_hbm, yidx_hbm,
    out,
    fbuf, mbuf, own_buf, x_own, x32, m32, far_s, far_r, side_s, side_r, hold, ax, gfx, gbx,
    send_z, recv_z, send_c, entering_all, send_y, recv_y, base, reach,
    lines, weights, mixed_all, smooth, acc, tab, lmat, vmat, square_work, vert, loc, xidx, alpha, yidx,
    local_sem, sm_s, sm_r, sz_s, sz_r, sc_s, sc_r, sy_s, sy_r, sx_s, sx_r,
):
    tile = lax.axis_index("tile")
    mem = lax.axis_index("mem")
    groups = tiles // SPAN
    q = lax.rem(tile, SPAN)
    y = tile // SPAN
    cols = field.shape[1]
    rows = field.shape[2]
    blocks = rows // LANES
    own = cols // mems
    levels = vert.shape[-1]
    padded = -(-slabs // 16) * 16
    pitch = x32.shape[1] // padded

    shift = (padded - slabs) * (mem // (mems - 1))
    get_own = pltpu.make_async_copy(
        field.at[pl.ds(16 * mem - shift, 16)], own_buf, local_sem.at[7]
    )
    get_own.start()

    barrier = pltpu.get_barrier_semaphore()

    for d in far_first(SPAN):
        pl.semaphore_signal(
            barrier,
            inc=1,
            device_id={"tile": y * SPAN + lax.rem(q + d, SPAN)},
            device_id_type=MESH,
        )

    for d in far_first(groups):
        pl.semaphore_signal(
            barrier,
            inc=1,
            device_id={"tile": lax.rem(y + d, groups) * SPAN + q},
            device_id_type=MESH,
        )

    for d in far_first(mems):
        pl.semaphore_signal(
            barrier, inc=1, device_id={"mem": lax.rem(mem + d, mems)}, device_id_type=MESH
        )

    small = [
        pltpu.make_async_copy(src, dst, local_sem.at[2 + at])
        for at, (src, dst) in enumerate(
            (
                (xidx_hbm, xidx),
                (alpha_hbm, alpha),
                (yidx_hbm, yidx),
                (loc_hbm, loc),
                (vert_hbm, vert),
            )
        )
    ]
    for copy in small:
        copy.start()
    get_field = pltpu.make_async_copy(field, fbuf, local_sem.at[1])
    get_field.start()
    get_members = pltpu.make_async_copy(members.at[0], mbuf, local_sem.at[0])
    get_members.start()

    for copy in small:
        copy.wait()
    sub = lax.broadcasted_iota(jnp.int32, (padded, LANES), 0)

    @pl.loop(0, blocks)
    def _(b):
        lane = pl.ds(pl.multiple_of(b * LANES, LANES), LANES)
        idx = xidx[:, lane]
        a = jnp.zeros(idx.shape, F32)
        for k in range(alpha.shape[0]):
            a = jnp.where(idx == k, alpha[k], a)
        wide = jnp.where(
            sub < levels,
            jnp.broadcast_to(a[0:1], (padded, LANES)),
            jnp.broadcast_to(a[1:2], (padded, LANES)),
        )
        fwd, back = gains(wide)
        ax[b] = wide
        gfx[b] = fwd
        gbx[b] = back

    def spread(src, dst, count, room):
        def put(view, s, i):
            for b in range(blocks):
                part = src[s, :, b * LANES : (b + 1) * LANES].astype(F32)
                view[b, i * pitch : i * pitch + cols, :] = part

        done = count // 8 * 8

        @pl.loop(0, count // 8)
        def _(g):
            at = pl.ds(pl.multiple_of(g * 8 * pitch, 8), 8 * pitch)
            view = dst.at[:, at, :]
            for i in range(8):
                put(view, 8 * g + i, i)

        for s in range(done, count):
            put(dst.at[:, done * pitch : room * pitch, :], s, s - done)
        for b in range(blocks):
            left = slice(count * pitch, room * pitch)
            dst[b, left, :] = jnp.zeros(((room - count) * pitch, LANES), F32)

    near = (lax.rem(mem + 1, mems), lax.rem(mem + mems - 1, mems))
    opposite = lax.rem(mem + 2, mems)
    halves = (slice(0, own // 2), slice(own // 2, own))

    def pass_far(side):
        return pltpu.make_async_remote_copy(
            src_ref=far_s.at[halves[side]],
            dst_ref=far_r.at[side],
            send_sem=sm_s.at[side],
            recv_sem=sm_r.at[side],
            device_id={"mem": near[side]},
            device_id_type=MESH,
        )

    def pass_near(side, half):
        return pltpu.make_async_remote_copy(
            src_ref=side_s.at[side, half],
            dst_ref=side_r.at[side, half],
            send_sem=sm_s.at[2 + 2 * side + half],
            recv_sem=sm_r.at[2 + 2 * side + half],
            device_id={"mem": near[side]},
            device_id_type=MESH,
        )

    wide_lanes = 2 * LANES
    half_own = own // 2

    def ensemble(peer, half, dst):
        @pl.loop(0, half_own)
        def _(k):
            col = peer * own + half * half_own + k
            for w in range(rows // wide_lanes):

                def column(src):
                    at = pl.ds(col, padded, stride=pitch)
                    return jnp.concatenate([src[2 * w, at, :], src[2 * w + 1, at, :]], axis=1)

                m = column(m32)
                scaled = (m * column(x32)).astype(BF16)
                term = m * jnp.dot(lmat[...], scaled, preferred_element_type=F32)
                dst[k, :, w * wide_lanes : (w + 1) * wide_lanes] = term.astype(dst.dtype)

    quads = padded // 16

    def local_states(b, p, src, first):
        at = pl.ds(pl.multiple_of(p * 16, 16), 16)
        a, fwd, back = ax[b, at, :], gfx[b, at, :], gbx[b, at, :]
        f = jnp.zeros((16, LANES), F32)
        states = []
        for c in range(cols):
            f = a * f + fwd * src[b, pl.ds(first * pitch + c, 16, stride=pitch), :]
            states.append(f)
        value = jnp.zeros((16, LANES), F32)
        backs = [None] * cols
        for c in reversed(range(cols)):
            value = a * value + back * states[c]
            backs[c] = value
        return states, backs

    def mine(values, k):
        value = values[k]
        for g in range(1, mems):
            value = jnp.where(mem == g, values[g * own + k], value)
        return value

    def to_span(src, dst, s_sem, r_sem, d):
        peer = lax.rem(q + d, SPAN)
        return pltpu.make_async_remote_copy(
            src_ref=src.at[peer],
            dst_ref=dst.at[q],
            send_sem=s_sem.at[peer],
            recv_sem=r_sem.at[q],
            device_id={"tile": y * SPAN + peer},
            device_id_type=MESH,
        )

    def from_span(src, dst, s_sem, r_sem, d):
        peer = lax.rem(q + d, SPAN)
        return pltpu.make_async_remote_copy(
            src_ref=src.at[peer],
            dst_ref=dst.at[peer],
            send_sem=s_sem.at[peer],
            recv_sem=r_sem.at[peer],
            device_id={"tile": y * SPAN + peer},
            device_id_type=MESH,
        )

    get_own.wait()
    spread(own_buf, x_own, 16, 16 + padded - slabs)

    @pl.loop(0, blocks)
    def _(b):
        states, backs = local_states(b, mem, x_own, shift)
        for h in range(2):
            part = slice(8 * h, 8 * h + 8)
            pair = jnp.concatenate([states[-1][part], backs[0][part]], axis=0)
            send_z[2 * b + h] = pair.astype(BF16)

    pl.semaphore_wait(barrier, (mems - 1) + (SPAN - 1) + (groups - 1))

    for d in far_first(SPAN):
        to_span(send_z, recv_z, sz_s, sz_r, d).start()

    recv_z[q] = send_z[q]

    extended(lmat, loc, slabs, square_work)
    extended(vmat, vert, slabs, square_work)
    get_field.wait()
    spread(fbuf, x32, slabs, padded)
    get_members.wait()
    spread(mbuf, m32, slabs, padded)
    for half in range(2):
        ensemble(opposite, half, far_s.at[halves[half]])
        pass_far(half).start()
    for side in range(2):
        ensemble(near[side], 1 - side, side_s.at[side, 1 - side])
        pass_near(side, 1 - side).start()

    zero = jnp.zeros((8, LANES), F32)
    piece_at = pl.ds(pl.multiple_of(mem * 16 + lax.rem(q, 2) * 8, 8), 8)
    a = ax[q // 2, piece_at, :]
    back = gbx[q // 2, piece_at, :]
    f = jnp.ones_like(a)
    states = []
    for c in range(cols):
        f = a * f
        states.append(f)
    cross = zero
    for c in reversed(range(cols)):
        cross = a * cross + back * states[c]
    decay = states[-1]
    square = decay * decay
    total, fade, far_decay = zero, jnp.ones_like(a), jnp.ones_like(a)
    for _ in range(SPAN):
        total = total + fade
        fade = fade * square
        far_decay = far_decay * decay
    far_cross = cross * total

    for d in far_first(SPAN):
        from_span(send_z, recv_z, sz_s, sz_r, d).wait_recv()

    def scan_span(f, b):
        enter_f, enter_b = [], [None] * SPAN
        pairs = [recv_z[i].astype(F32) for i in range(SPAN)]
        for i in range(SPAN):
            enter_f.append(f)
            f = pairs[i][0:8] + decay * f
        for i in reversed(range(SPAN)):
            enter_b[i] = b
            b = pairs[i][8:16] + cross * enter_f[i] + decay * b
        return f, b, enter_f, enter_b

    end, begin, _, _ = scan_span(zero, zero)
    send_y[...] = jnp.concatenate([end, begin], axis=0).astype(BF16)

    def to_group(d):
        peer = lax.rem(y + d, groups)
        return pltpu.make_async_remote_copy(
            src_ref=send_y,
            dst_ref=recv_y.at[y],
            send_sem=sy_s.at[peer],
            recv_sem=sy_r.at[y],
            device_id={"tile": peer * SPAN + q},
            device_id_type=MESH,
        )

    def from_group(d):
        peer = lax.rem(y + d, groups)
        return pltpu.make_async_remote_copy(
            src_ref=send_y,
            dst_ref=recv_y.at[peer],
            send_sem=sy_s.at[peer],
            recv_sem=sy_r.at[peer],
            device_id={"tile": peer * SPAN + q},
            device_id_type=MESH,
        )

    for d in far_first(groups):
        to_group(d).start()

    recv_y[y] = send_y[...]

    @pl.loop(0, blocks)
    def _(b):
        @pl.loop(0, quads)
        def _(p):
            _, backs = local_states(b, p, x32, p * 16)
            at = pl.ds(pl.multiple_of(b * padded + p * 16, 16), 16)
            for k in range(own):
                base[k, at, :] = mine(backs, k)

        for kind in range(2):
            at = slice(0, 16) if kind == 0 else slice(padded - 16, padded)
            a, back = ax[b, at, :], gbx[b, at, :]
            f = jnp.ones((16, LANES), F32)
            states = []
            for c in range(cols):
                f = a * f
                states.append(f)
            value = jnp.zeros((16, LANES), F32)
            backs = [None] * cols
            for c in reversed(range(cols)):
                value = a * value + back * states[c]
                backs[c] = value
            for k in range(own):
                reach[kind, b, 2 * k] = mine(backs, k)
                reach[kind, b, 2 * k + 1] = mine(states[::-1], k)

    for d in far_first(groups):
        from_group(d).wait_recv()

    pairs = [recv_y[i].astype(F32) for i in range(groups)]
    enter = []
    f = zero
    mine_f = zero
    for i in range(groups):
        enter.append(f)
        mine_f = jnp.where(y == i, f, mine_f)
        f = pairs[i][0:8] + far_decay * f
    b = zero
    mine_b = zero
    for i in reversed(range(groups)):
        mine_b = jnp.where(y == i, b, mine_b)
        b = pairs[i][8:16] + far_cross * enter[i] + far_decay * b
    _, _, enter_f, enter_b = scan_span(mine_f, mine_b)
    for i in range(SPAN):
        send_c[i] = jnp.concatenate([enter_f[i], enter_b[i]], axis=0).astype(BF16)

    recv_c = entering_all.at[mem]

    for d in far_first(SPAN):
        to_span(send_c, recv_c, sc_s, sc_r, d).start()

    entering_all[mem, q] = send_c[q]

    for side in range(2):
        ensemble(near[side], side, hold.at[side])
    for side in range(2):
        pass_far(side).wait_recv()

        @pl.loop(0, half_own)
        def _(k):
            total = hold[side, k] + far_r[side, k].astype(F32)
            side_s[side, side, k] = total.astype(BF16)

        pass_near(side, side).start()

    for half in range(2):
        ensemble(mem, half, acc.at[halves[half]])

    chunk = SPAN // 4

    def gather(d, c, source):
        at = entering_all.at[source, pl.ds(c * chunk, chunk)]
        return pltpu.make_async_remote_copy(
            src_ref=at,
            dst_ref=at,
            send_sem=sx_s.at[d, c],
            recv_sem=sx_r.at[d, c],
            device_id={"mem": lax.rem(mem + d, mems)},
            device_id_type=MESH,
        )

    for i in (0, 1, 3, 2):
        c = lax.rem(q // chunk + i, 4)
        for r in range(chunk):
            piece = c * chunk + r

            def returned(piece=piece):
                pltpu.make_async_remote_copy(
                    src_ref=send_c.at[piece],
                    dst_ref=recv_c.at[piece],
                    send_sem=sc_s.at[piece],
                    recv_sem=sc_r.at[piece],
                    device_id={"tile": y * SPAN + piece},
                    device_id_type=MESH,
                ).wait_recv()

            if i == 0:
                pl.when(piece != q)(returned)
            else:
                returned()
        for d in (2, 1, 3):
            gather(d, c, mem).start()

    lane8 = lax.broadcasted_iota(jnp.int32, (8, LANES), 1)
    sub8 = lax.broadcasted_iota(jnp.int32, (8, LANES), 0)
    row_i = lax.broadcasted_iota(jnp.int32, (LANES, LANES), 0)
    row_j = lax.broadcasted_iota(jnp.int32, (LANES, LANES), 1)

    def geometric(count, ratio):
        value = jnp.zeros(count.shape, F32)
        reached = jnp.ones(count.shape, F32)
        part = jnp.float32(1.0)
        for bit in range(8):
            has = (count & (1 << bit)) != 0
            value = jnp.where(has, value + reached * part, value)
            reached = jnp.where(has, reached * ratio, reached)
            part = part * (1.0 + ratio)
            ratio = ratio * ratio
        return value

    @pl.loop(0, own)
    def _(c):
        col = tile * cols + mem * own + c
        tables = []
        for kind in range(2):
            coeff = alpha[yidx[kind, col]]
            a = jnp.full((8, LANES), coeff, F32)
            fwd, back = gains(a)
            rate = jnp.log(jnp.maximum(a, 1e-37))

            def tall(x):
                return jnp.broadcast_to(x[0:1], (LANES, LANES))

            def power(exponent, log_a):
                return jnp.exp(exponent.astype(F32) * log_a)

            ratio = coeff * coeff
            inner = power(jnp.abs(row_i - row_j), tall(rate)) * tall(fwd * back)
            inner = inner * geometric(LANES - jnp.maximum(row_i, row_j), ratio)
            ends = power(LANES - 1 - row_i, tall(rate)) * tall(fwd)
            starts = jnp.broadcast_to(inner[:, 0:1], (LANES, LANES))
            for at, part in enumerate((inner, ends, starts)):
                high = part.astype(BF16)
                low = (part - high.astype(F32)).astype(BF16)
                lane = slice(at * LANES, (at + 1) * LANES)
                weights[2 * c + kind, 0:LANES, lane] = high
                weights[2 * c + kind, LANES : 2 * LANES, lane] = low
            far = coeff
            for _ in range(7):
                far = far * far
            whole = geometric(jnp.full((8, LANES), LANES, jnp.int32), ratio)
            tables.append(
                (
                    back * power(lane8 + 1, rate) * geometric(LANES - lane8, ratio),
                    power(LANES - lane8, rate),
                    jnp.full((8, LANES), far, F32),
                    back * a * whole,
                )
            )
        for at, (first, second) in enumerate(zip(*tables)):
            tab[2 * c, at] = first
            tab[2 * c + 1, at] = jnp.where(sub8 < levels % 8, first, second)

    def add_carries(p):
        kind = p // (quads - 1)
        for b in range(blocks):
            low = entering_all[p, 2 * b].astype(F32)
            high = entering_all[p, 2 * b + 1].astype(F32)
            f = jnp.concatenate([low[0:8], high[0:8]], axis=0)
            bk = jnp.concatenate([low[8:16], high[8:16]], axis=0)
            at = pl.ds(pl.multiple_of(b * padded + p * 16, 16), 16)
            for k in range(own):
                value = base[k, at, :] + reach[kind, b, 2 * k] * f + reach[kind, b, 2 * k + 1] * bk
                lines[k, at, :] = value.astype(BF16)

    add_carries(mem)
    for d in (1, 3, 2):
        source = lax.rem(mem + mems - d, mems)
        for c in range(4):
            gather(d, c, source).wait_recv()
        add_carries(source)

    for side in range(2):
        for half in range(2):
            pass_near(side, half).wait_recv()

    last = padded - 8

    for c in range(own):
        x = jnp.concatenate([lines[c], lines[c]], axis=1)
        mixed = mixed_all.at[c % 2]
        mixed[...] = jnp.dot(x, weights[2 * c], preferred_element_type=F32)
        tail = jnp.concatenate(
            [lines[c, (b + 1) * padded - 16 : (b + 1) * padded, :] for b in range(blocks)], axis=0
        )
        tail = jnp.concatenate([tail, tail], axis=1)
        other = jnp.dot(tail, weights[2 * c + 1], preferred_element_type=F32)
        pick = jnp.concatenate([sub8] * 3, axis=1) < levels % 8
        for b in range(blocks):
            at = slice(b * padded + last, (b + 1) * padded)
            mixed[at, :] = jnp.where(pick, mixed[at, :], other[16 * b + 8 : 16 * b + 16])

        for g in range(padded // 8):
            t = 2 * c + g // (levels // 8)
            from_left, from_right, far, cross = tab[t, 0], tab[t, 1], tab[t, 2], tab[t, 3]

            def block(b, part):
                at = slice(b * padded + g * 8, b * padded + g * 8 + 8)
                return mixed[at, part * LANES : (part + 1) * LANES]

            state = jnp.zeros((8, LANES), F32)
            entering = []
            for b in range(blocks):
                entering.append(state)
                state = block(b, 1) + far * state
            state = jnp.zeros((8, LANES), F32)
            for b in reversed(range(blocks)):
                value = block(b, 0) + from_left * entering[b] + from_right * state
                smooth[c, g * 8 : g * 8 + 8, b * LANES : (b + 1) * LANES] = value
                state = block(b, 2) + cross * entering[b] + far * state

        for w in range(rows // wide_lanes):
            lane = slice(w * wide_lanes, (w + 1) * wide_lanes)
            others = side_r[0, c // half_own, c % half_own, :, lane].astype(F32)
            others = others + side_r[1, c // half_own, c % half_own, :, lane].astype(F32)
            x = smooth[c, :, lane].astype(BF16)
            static = jnp.dot(vmat[...], x, preferred_element_type=F32)
            out[c, :, lane] = (static + (acc[c, :, lane] + others) / (mems - 1)).astype(BF16)

    for d in (1, 2, 3):
        for c in range(4):
            gather(d, c, mem).wait_send()
    for side in range(2):
        pass_far(side).wait_send()
        for half in range(2):
            pass_near(side, half).wait_send()

    for d in far_first(SPAN):
        to_span(send_z, recv_z, sz_s, sz_r, d).wait_send()
        to_span(send_c, recv_c, sc_s, sc_r, d).wait_send()

    for d in far_first(groups):
        to_group(d).wait_send()


def body(tiles, mems, field, vert, loc, alpha, xidx, yidx, members):
    slabs, cols, rows = field.shape
    own = cols // mems
    padded = -(-slabs // 16) * 16
    blocks = rows // LANES
    groups = tiles // SPAN
    dma = pltpu.SemaphoreType.DMA
    vmem = pltpu.VMEM
    result = pl.pallas_call(
        functools.partial(kernel, tiles, mems, slabs),
        out_shape=jax.ShapeDtypeStruct((own, padded, rows), BF16),
        in_specs=[pl.BlockSpec(memory_space=pl.ANY)] * 7,
        out_specs=pl.BlockSpec(memory_space=pltpu.VMEM),
        scratch_shapes=[
            vmem((slabs, cols, rows), BF16),
            vmem((slabs, cols, rows), BF16),
            vmem((16, cols, rows), BF16),
            vmem((blocks, -(-(16 + padded - slabs) * (cols + 1) // 8) * 8, LANES), F32),
            vmem((blocks, padded * (cols + 1), LANES), F32),
            vmem((blocks, padded * (cols + 1), LANES), F32),
            vmem((own, padded, rows), BF16),
            vmem((2, own // 2, padded, rows), BF16),
            vmem((2, 2, own // 2, padded, rows), BF16),
            vmem((2, 2, own // 2, padded, rows), BF16),
            vmem((2, own // 2, padded, rows), F32),
            vmem((blocks, padded, LANES), F32),
            vmem((blocks, padded, LANES), F32),
            vmem((blocks, padded, LANES), F32),
            vmem((SPAN, 16, LANES), BF16),
            vmem((SPAN, 16, LANES), BF16),
            vmem((SPAN, 16, LANES), BF16),
            vmem((mems, SPAN, 16, LANES), BF16),
            vmem((16, LANES), BF16),
            vmem((groups, 16, LANES), BF16),
            vmem((own, blocks * padded, LANES), F32),
            vmem((2, blocks, 2 * own, 16, LANES), F32),
            vmem((own, blocks * padded, LANES), BF16),
            vmem((2 * own, 2 * LANES, 3 * LANES), BF16),
            vmem((2, blocks * padded, 3 * LANES), F32),
            vmem((own, padded, rows), F32),
            vmem((own, padded, rows), F32),
            vmem((2 * own, 4, 8, LANES), F32),
            vmem((padded, padded), BF16),
            vmem((padded, padded), BF16),
            vmem((padded, padded), F32),
            vmem(vert.shape, vert.dtype),
            vmem(loc.shape, loc.dtype),
            vmem(xidx.shape, xidx.dtype),
            pltpu.SMEM(alpha.shape, alpha.dtype),
            pltpu.SMEM(yidx.shape, yidx.dtype),
            dma((8,)),
            dma((6,)),
            dma((6,)),
            dma((SPAN,)),
            dma((SPAN,)),
            dma((SPAN,)),
            dma((SPAN,)),
            dma((groups,)),
            dma((groups,)),
            dma((mems, 4)),
            dma((mems, 4)),
        ],
        compiler_params=pltpu.CompilerParams(
            collective_id=0, has_side_effects=True, vmem_limit_bytes=60 * 2**20
        ),
    )(field, members, vert, loc, xidx, alpha, yidx)
    return jnp.swapaxes(result, 0, 1)[:slabs]


def solution(mesh):
    return jax.shard_map(
        functools.partial(body, mesh.shape["tile"], mesh.shape["mem"]),
        mesh=mesh,
        in_specs=(P(None, "tile", None), P(), P(), P(), P(), P(), P("mem", None, "tile", None)),
        out_specs=P(None, ("tile", "mem"), None),
        check_vma=False,
    )
```

```python
import functools

import jax
import jax.numpy as jnp
from jax import lax
from jax.experimental import pallas as pl
from jax.experimental.pallas import tpu as pltpu
from jax.sharding import PartitionSpec as P

MESH = pl.DeviceIdType.MESH
F32 = jnp.float32
BF16 = jnp.bfloat16
LANES = 128
SPAN = 16


def far_first(size):
    return sorted(range(1, size), key=lambda d: abs(2 * d - size))


def gains(a):
    return jnp.sqrt(1.0 - a * a), (1.0 - a * a) / jnp.sqrt(1.0 + a * a)


def extended(dst, matrix, pad, work):
    n = matrix.shape[-1]
    work[...] = jnp.zeros(work.shape, F32)
    work[0:n, 0:n] = matrix[0].astype(F32)
    i = lax.broadcasted_iota(jnp.int32, dst.shape, 0)
    j = lax.broadcasted_iota(jnp.int32, dst.shape, 1)
    keep = (i == j) & (i >= n) & (i < pad)
    dst[...] = jnp.where(keep, 1.0, work[...]).astype(BF16)


def kernel(
    tiles, mems, slabs,
    field, members, vert_hbm, loc_hbm, xidx_hbm, alpha_hbm, yidx_hbm,
    out,
    fbuf, mbuf, own_buf, x_own, x32, m32, far_s, far_r, side_s, side_r, hold, ax, gfx, gbx,
    send_z, recv_z, send_c, entering_all, send_y, recv_y, base, reach,
    lines, weights, mixed_all, smooth, acc, tab, lmat, vmat, square_work, vert, loc, xidx, alpha, yidx,
    local_sem, sm_s, sm_r, sz_s, sz_r, sc_s, sc_r, sy_s, sy_r, sx_s, sx_r,
):
    tile = lax.axis_index("tile")
    mem = lax.axis_index("mem")
    groups = tiles // SPAN
    q = lax.rem(tile, SPAN)
    y = tile // SPAN
    cols = field.shape[1]
    rows = field.shape[2]
    blocks = rows // LANES
    own = cols // mems
    levels = vert.shape[-1]
    padded = -(-slabs // 16) * 16
    pitch = x32.shape[1] // padded

    shift = (padded - slabs) * (mem // (mems - 1))
    get_own = pltpu.make_async_copy(
        field.at[pl.ds(16 * mem - shift, 16)], own_buf, local_sem.at[7]
    )
    get_own.start()

    barrier = pltpu.get_barrier_semaphore()

    for d in far_first(SPAN):
        pl.semaphore_signal(
            barrier,
            inc=1,
            device_id={"tile": y * SPAN + lax.rem(q + d, SPAN)},
            device_id_type=MESH,
        )

    for d in far_first(groups):
        pl.semaphore_signal(
            barrier,
            inc=1,
            device_id={"tile": lax.rem(y + d, groups) * SPAN + q},
            device_id_type=MESH,
        )

    for d in far_first(mems):
        pl.semaphore_signal(
            barrier, inc=1, device_id={"mem": lax.rem(mem + d, mems)}, device_id_type=MESH
        )

    small = [
        pltpu.make_async_copy(src, dst, local_sem.at[2 + at])
        for at, (src, dst) in enumerate(
            (
                (xidx_hbm, xidx),
                (alpha_hbm, alpha),
                (yidx_hbm, yidx),
                (loc_hbm, loc),
                (vert_hbm, vert),
            )
        )
    ]
    for copy in small:
        copy.start()
    get_field = pltpu.make_async_copy(field, fbuf, local_sem.at[1])
    get_field.start()
    get_members = pltpu.make_async_copy(members.at[0], mbuf, local_sem.at[0])
    get_members.start()

    for copy in small:
        copy.wait()
    sub = lax.broadcasted_iota(jnp.int32, (padded, LANES), 0)

    @pl.loop(0, blocks)
    def _(b):
        lane = pl.ds(pl.multiple_of(b * LANES, LANES), LANES)
        idx = xidx[:, lane]
        a = jnp.zeros(idx.shape, F32)
        for k in range(alpha.shape[0]):
            a = jnp.where(idx == k, alpha[k], a)
        wide = jnp.where(
            sub < levels,
            jnp.broadcast_to(a[0:1], (padded, LANES)),
            jnp.broadcast_to(a[1:2], (padded, LANES)),
        )
        fwd, back = gains(wide)
        ax[b] = wide
        gfx[b] = fwd
        gbx[b] = back

    def spread(src, dst, count, room):
        def put(view, s, i):
            for b in range(blocks):
                part = src[s, :, b * LANES : (b + 1) * LANES].astype(F32)
                view[b, i * pitch : i * pitch + cols, :] = part

        done = count // 8 * 8

        @pl.loop(0, count // 8)
        def _(g):
            at = pl.ds(pl.multiple_of(g * 8 * pitch, 8), 8 * pitch)
            view = dst.at[:, at, :]
            for i in range(8):
                put(view, 8 * g + i, i)

        for s in range(done, count):
            put(dst.at[:, done * pitch : room * pitch, :], s, s - done)
        for b in range(blocks):
            left = slice(count * pitch, room * pitch)
            dst[b, left, :] = jnp.zeros(((room - count) * pitch, LANES), F32)

    near = (lax.rem(mem + 1, mems), lax.rem(mem + mems - 1, mems))
    opposite = lax.rem(mem + 2, mems)
    halves = (slice(0, own // 2), slice(own // 2, own))

    def pass_far(side):
        return pltpu.make_async_remote_copy(
            src_ref=far_s.at[halves[side]],
            dst_ref=far_r.at[side],
            send_sem=sm_s.at[side],
            recv_sem=sm_r.at[side],
            device_id={"mem": near[side]},
            device_id_type=MESH,
        )

    def pass_near(side, half):
        return pltpu.make_async_remote_copy(
            src_ref=side_s.at[side, half],
            dst_ref=side_r.at[side, half],
            send_sem=sm_s.at[2 + 2 * side + half],
            recv_sem=sm_r.at[2 + 2 * side + half],
            device_id={"mem": near[side]},
            device_id_type=MESH,
        )

    wide_lanes = 2 * LANES
    half_own = own // 2

    def ensemble(peer, half, dst):
        @pl.loop(0, half_own)
        def _(k):
            col = peer * own + half * half_own + k
            for w in range(rows // wide_lanes):

                def column(src):
                    at = pl.ds(col, padded, stride=pitch)
                    return jnp.concatenate([src[2 * w, at, :], src[2 * w + 1, at, :]], axis=1)

                m = column(m32)
                scaled = (m * column(x32)).astype(BF16)
                term = m * jnp.dot(lmat[...], scaled, preferred_element_type=F32)
                dst[k, :, w * wide_lanes : (w + 1) * wide_lanes] = term.astype(dst.dtype)

    quads = padded // 16

    def local_states(b, p, src, first):
        at = pl.ds(pl.multiple_of(p * 16, 16), 16)
        a, fwd, back = ax[b, at, :], gfx[b, at, :], gbx[b, at, :]
        f = jnp.zeros((16, LANES), F32)
        states = []
        for c in range(cols):
            f = a * f + fwd * src[b, pl.ds(first * pitch + c, 16, stride=pitch), :]
            states.append(f)
        value = jnp.zeros((16, LANES), F32)
        backs = [None] * cols
        for c in reversed(range(cols)):
            value = a * value + back * states[c]
            backs[c] = value
        return states, backs

    def mine(values, k):
        value = values[k]
        for g in range(1, mems):
            value = jnp.where(mem == g, values[g * own + k], value)
        return value

    def to_span(src, dst, s_sem, r_sem, d):
        peer = lax.rem(q + d, SPAN)
        return pltpu.make_async_remote_copy(
            src_ref=src.at[peer],
            dst_ref=dst.at[q],
            send_sem=s_sem.at[peer],
            recv_sem=r_sem.at[q],
            device_id={"tile": y * SPAN + peer},
            device_id_type=MESH,
        )

    def from_span(src, dst, s_sem, r_sem, d):
        peer = lax.rem(q + d, SPAN)
        return pltpu.make_async_remote_copy(
            src_ref=src.at[peer],
            dst_ref=dst.at[peer],
            send_sem=s_sem.at[peer],
            recv_sem=r_sem.at[peer],
            device_id={"tile": y * SPAN + peer},
            device_id_type=MESH,
        )

    get_own.wait()
    spread(own_buf, x_own, 16, 16 + padded - slabs)

    @pl.loop(0, blocks)
    def _(b):
        states, backs = local_states(b, mem, x_own, shift)
        for h in range(2):
            part = slice(8 * h, 8 * h + 8)
            pair = jnp.concatenate([states[-1][part], backs[0][part]], axis=0)
            send_z[2 * b + h] = pair.astype(BF16)

    pl.semaphore_wait(barrier, (mems - 1) + (SPAN - 1) + (groups - 1))

    for d in far_first(SPAN):
        to_span(send_z, recv_z, sz_s, sz_r, d).start()

    recv_z[q] = send_z[q]

    extended(lmat, loc, slabs, square_work)
    extended(vmat, vert, slabs, square_work)
    get_field.wait()
    spread(fbuf, x32, slabs, padded)
    get_members.wait()
    spread(mbuf, m32, slabs, padded)
    for half in range(2):
        ensemble(opposite, half, far_s.at[halves[half]])
        pass_far(half).start()
    for side in range(2):
        ensemble(near[side], 1 - side, side_s.at[side, 1 - side])
        pass_near(side, 1 - side).start()

    zero = jnp.zeros((8, LANES), F32)
    piece_at = pl.ds(pl.multiple_of(mem * 16 + lax.rem(q, 2) * 8, 8), 8)
    a = ax[q // 2, piece_at, :]
    back = gbx[q // 2, piece_at, :]
    f = jnp.ones_like(a)
    states = []
    for c in range(cols):
        f = a * f
        states.append(f)
    cross = zero
    for c in reversed(range(cols)):
        cross = a * cross + back * states[c]
    decay = states[-1]
    square = decay * decay
    total, fade, far_decay = zero, jnp.ones_like(a), jnp.ones_like(a)
    for _ in range(SPAN):
        total = total + fade
        fade = fade * square
        far_decay = far_decay * decay
    far_cross = cross * total

    for d in far_first(SPAN):
        from_span(send_z, recv_z, sz_s, sz_r, d).wait_recv()

    def scan_span(f, b):
        enter_f, enter_b = [], [None] * SPAN
        pairs = [recv_z[i].astype(F32) for i in range(SPAN)]
        for i in range(SPAN):
            enter_f.append(f)
            f = pairs[i][0:8] + decay * f
        for i in reversed(range(SPAN)):
            enter_b[i] = b
            b = pairs[i][8:16] + cross * enter_f[i] + decay * b
        return f, b, enter_f, enter_b

    end, begin, _, _ = scan_span(zero, zero)
    send_y[...] = jnp.concatenate([end, begin], axis=0).astype(BF16)

    def to_group(d):
        peer = lax.rem(y + d, groups)
        return pltpu.make_async_remote_copy(
            src_ref=send_y,
            dst_ref=recv_y.at[y],
            send_sem=sy_s.at[peer],
            recv_sem=sy_r.at[y],
            device_id={"tile": peer * SPAN + q},
            device_id_type=MESH,
        )

    def from_group(d):
        peer = lax.rem(y + d, groups)
        return pltpu.make_async_remote_copy(
            src_ref=send_y,
            dst_ref=recv_y.at[peer],
            send_sem=sy_s.at[peer],
            recv_sem=sy_r.at[peer],
            device_id={"tile": peer * SPAN + q},
            device_id_type=MESH,
        )

    for d in far_first(groups):
        to_group(d).start()

    recv_y[y] = send_y[...]

    @pl.loop(0, blocks)
    def _(b):
        @pl.loop(0, quads)
        def _(p):
            _, backs = local_states(b, p, x32, p * 16)
            at = pl.ds(pl.multiple_of(b * padded + p * 16, 16), 16)
            for k in range(own):
                base[k, at, :] = mine(backs, k)

        for kind in range(2):
            at = slice(0, 16) if kind == 0 else slice(padded - 16, padded)
            a, back = ax[b, at, :], gbx[b, at, :]
            f = jnp.ones((16, LANES), F32)
            states = []
            for c in range(cols):
                f = a * f
                states.append(f)
            value = jnp.zeros((16, LANES), F32)
            backs = [None] * cols
            for c in reversed(range(cols)):
                value = a * value + back * states[c]
                backs[c] = value
            for k in range(own):
                reach[kind, b, 2 * k] = mine(backs, k)
                reach[kind, b, 2 * k + 1] = mine(states[::-1], k)

    for d in far_first(groups):
        from_group(d).wait_recv()

    pairs = [recv_y[i].astype(F32) for i in range(groups)]
    enter = []
    f = zero
    mine_f = zero
    for i in range(groups):
        enter.append(f)
        mine_f = jnp.where(y == i, f, mine_f)
        f = pairs[i][0:8] + far_decay * f
    b = zero
    mine_b = zero
    for i in reversed(range(groups)):
        mine_b = jnp.where(y == i, b, mine_b)
        b = pairs[i][8:16] + far_cross * enter[i] + far_decay * b
    _, _, enter_f, enter_b = scan_span(mine_f, mine_b)
    for i in range(SPAN):
        send_c[i] = jnp.concatenate([enter_f[i], enter_b[i]], axis=0).astype(BF16)

    recv_c = entering_all.at[mem]

    for d in far_first(SPAN):
        to_span(send_c, recv_c, sc_s, sc_r, d).start()

    entering_all[mem, q] = send_c[q]

    for side in range(2):
        ensemble(near[side], side, hold.at[side])
    for side in range(2):
        pass_far(side).wait_recv()

        @pl.loop(0, half_own)
        def _(k):
            total = hold[side, k] + far_r[side, k].astype(F32)
            side_s[side, side, k] = total.astype(BF16)

        pass_near(side, side).start()

    for half in range(2):
        ensemble(mem, half, acc.at[halves[half]])

    chunk = SPAN // 4

    def gather(d, c, source):
        at = entering_all.at[source, pl.ds(c * chunk, chunk)]
        return pltpu.make_async_remote_copy(
            src_ref=at,
            dst_ref=at,
            send_sem=sx_s.at[d, c],
            recv_sem=sx_r.at[d, c],
            device_id={"mem": lax.rem(mem + d, mems)},
            device_id_type=MESH,
        )

    for i in (0, 1, 3, 2):
        c = lax.rem(q // chunk + i, 4)
        for r in range(chunk):
            piece = c * chunk + r

            def returned(piece=piece):
                pltpu.make_async_remote_copy(
                    src_ref=send_c.at[piece],
                    dst_ref=recv_c.at[piece],
                    send_sem=sc_s.at[piece],
                    recv_sem=sc_r.at[piece],
                    device_id={"tile": y * SPAN + piece},
                    device_id_type=MESH,
                ).wait_recv()

            if i == 0:
                pl.when(piece != q)(returned)
            else:
                returned()
        for d in (2, 1, 3):
            gather(d, c, mem).start()

    lane8 = lax.broadcasted_iota(jnp.int32, (8, LANES), 1)
    sub8 = lax.broadcasted_iota(jnp.int32, (8, LANES), 0)
    row_i = lax.broadcasted_iota(jnp.int32, (LANES, LANES), 0)
    row_j = lax.broadcasted_iota(jnp.int32, (LANES, LANES), 1)

    def geometric(count, ratio):
        value = jnp.zeros(count.shape, F32)
        reached = jnp.ones(count.shape, F32)
        part = jnp.float32(1.0)
        for bit in range(8):
            has = (count & (1 << bit)) != 0
            value = jnp.where(has, value + reached * part, value)
            reached = jnp.where(has, reached * ratio, reached)
            part = part * (1.0 + ratio)
            ratio = ratio * ratio
        return value

    @pl.loop(0, own)
    def _(c):
        col = tile * cols + mem * own + c
        tables = []
        for kind in range(2):
            coeff = alpha[yidx[kind, col]]
            a = jnp.full((8, LANES), coeff, F32)
            fwd, back = gains(a)
            rate = jnp.log(jnp.maximum(a, 1e-37))

            def tall(x):
                return jnp.broadcast_to(x[0:1], (LANES, LANES))

            def power(exponent, log_a):
                return jnp.exp(exponent.astype(F32) * log_a)

            ratio = coeff * coeff
            inner = power(jnp.abs(row_i - row_j), tall(rate)) * tall(fwd * back)
            inner = inner * geometric(LANES - jnp.maximum(row_i, row_j), ratio)
            ends = power(LANES - 1 - row_i, tall(rate)) * tall(fwd)
            starts = jnp.broadcast_to(inner[:, 0:1], (LANES, LANES))
            for at, part in enumerate((inner, ends, starts)):
                high = part.astype(BF16)
                low = (part - high.astype(F32)).astype(BF16)
                lane = slice(at * LANES, (at + 1) * LANES)
                weights[2 * c + kind, 0:LANES, lane] = high
                weights[2 * c + kind, LANES : 2 * LANES, lane] = low
            far = coeff
            for _ in range(7):
                far = far * far
            whole = geometric(jnp.full((8, LANES), LANES, jnp.int32), ratio)
            tables.append(
                (
                    back * power(lane8 + 1, rate) * geometric(LANES - lane8, ratio),
                    power(LANES - lane8, rate),
                    jnp.full((8, LANES), far, F32),
                    back * a * whole,
                )
            )
        for at, (first, second) in enumerate(zip(*tables)):
            tab[2 * c, at] = first
            tab[2 * c + 1, at] = jnp.where(sub8 < levels % 8, first, second)

    def add_carries(p):
        kind = p // (quads - 1)
        for b in range(blocks):
            low = entering_all[p, 2 * b].astype(F32)
            high = entering_all[p, 2 * b + 1].astype(F32)
            f = jnp.concatenate([low[0:8], high[0:8]], axis=0)
            bk = jnp.concatenate([low[8:16], high[8:16]], axis=0)
            at = pl.ds(pl.multiple_of(b * padded + p * 16, 16), 16)
            for k in range(own):
                value = base[k, at, :] + reach[kind, b, 2 * k] * f + reach[kind, b, 2 * k + 1] * bk
                lines[k, at, :] = value.astype(BF16)

    add_carries(mem)
    for d in (1, 3, 2):
        source = lax.rem(mem + mems - d, mems)
        for c in range(4):
            gather(d, c, source).wait_recv()
        add_carries(source)

    for side in range(2):
        for half in range(2):
            pass_near(side, half).wait_recv()

    last = padded - 8

    for c in range(own):
        x = jnp.concatenate([lines[c], lines[c]], axis=1)
        mixed = mixed_all.at[c % 2]
        mixed[...] = jnp.dot(x, weights[2 * c], preferred_element_type=F32)
        tail = jnp.concatenate(
            [lines[c, (b + 1) * padded - 16 : (b + 1) * padded, :] for b in range(blocks)], axis=0
        )
        tail = jnp.concatenate([tail, tail], axis=1)
        other = jnp.dot(tail, weights[2 * c + 1], preferred_element_type=F32)
        pick = jnp.concatenate([sub8] * 3, axis=1) < levels % 8
        for b in range(blocks):
            at = slice(b * padded + last, (b + 1) * padded)
            mixed[at, :] = jnp.where(pick, mixed[at, :], other[16 * b + 8 : 16 * b + 16])

        for g in range(padded // 8):
            t = 2 * c + g // (levels // 8)
            from_left, from_right, far, cross = tab[t, 0], tab[t, 1], tab[t, 2], tab[t, 3]

            def block(b, part):
                at = slice(b * padded + g * 8, b * padded + g * 8 + 8)
                return mixed[at, part * LANES : (part + 1) * LANES]

            state = jnp.zeros((8, LANES), F32)
            entering = []
            for b in range(blocks):
                entering.append(state)
                state = block(b, 1) + far * state
            state = jnp.zeros((8, LANES), F32)
            for b in reversed(range(blocks)):
                value = block(b, 0) + from_left * entering[b] + from_right * state
                smooth[c, g * 8 : g * 8 + 8, b * LANES : (b + 1) * LANES] = value
                state = block(b, 2) + cross * entering[b] + far * state

        for w in range(rows // wide_lanes):
            lane = slice(w * wide_lanes, (w + 1) * wide_lanes)
            others = side_r[0, c // half_own, c % half_own, :, lane].astype(F32)
            others = others + side_r[1, c // half_own, c % half_own, :, lane].astype(F32)
            x = smooth[c, :, lane].astype(BF16)
            static = jnp.dot(vmat[...], x, preferred_element_type=F32)
            out[c, :, lane] = (static + (acc[c, :, lane] + others) / (mems - 1)).astype(BF16)

    for d in (1, 2, 3):
        for c in range(4):
            gather(d, c, mem).wait_send()
    for side in range(2):
        pass_far(side).wait_send()
        for half in range(2):
            pass_near(side, half).wait_send()

    for d in far_first(SPAN):
        to_span(send_z, recv_z, sz_s, sz_r, d).wait_send()
        to_span(send_c, recv_c, sc_s, sc_r, d).wait_send()

    for d in far_first(groups):
        to_group(d).wait_send()


def body(tiles, mems, field, vert, loc, alpha, xidx, yidx, members):
    slabs, cols, rows = field.shape
    own = cols // mems
    padded = -(-slabs // 16) * 16
    blocks = rows // LANES
    groups = tiles // SPAN
    dma = pltpu.SemaphoreType.DMA
    vmem = pltpu.VMEM
    operands = [
        pltpu.with_memory_space_constraint(x, pltpu.HBM)
        for x in (field, members, vert, loc, xidx, alpha, yidx)
    ]
    result = pl.pallas_call(
        functools.partial(kernel, tiles, mems, slabs),
        out_shape=jax.ShapeDtypeStruct((own, padded, rows), BF16),
        in_specs=[pl.BlockSpec(memory_space=pl.ANY)] * 7,
        out_specs=pl.BlockSpec(memory_space=pltpu.VMEM),
        scratch_shapes=[
            vmem((slabs, cols, rows), BF16),
            vmem((slabs, cols, rows), BF16),
            vmem((16, cols, rows), BF16),
            vmem((blocks, -(-(16 + padded - slabs) * (cols + 1) // 8) * 8, LANES), F32),
            vmem((blocks, padded * (cols + 1), LANES), F32),
            vmem((blocks, padded * (cols + 1), LANES), F32),
            vmem((own, padded, rows), BF16),
            vmem((2, own // 2, padded, rows), BF16),
            vmem((2, 2, own // 2, padded, rows), BF16),
            vmem((2, 2, own // 2, padded, rows), BF16),
            vmem((2, own // 2, padded, rows), F32),
            vmem((blocks, padded, LANES), F32),
            vmem((blocks, padded, LANES), F32),
            vmem((blocks, padded, LANES), F32),
            vmem((SPAN, 16, LANES), BF16),
            vmem((SPAN, 16, LANES), BF16),
            vmem((SPAN, 16, LANES), BF16),
            vmem((mems, SPAN, 16, LANES), BF16),
            vmem((16, LANES), BF16),
            vmem((groups, 16, LANES), BF16),
            vmem((own, blocks * padded, LANES), F32),
            vmem((2, blocks, 2 * own, 16, LANES), F32),
            vmem((own, blocks * padded, LANES), BF16),
            vmem((2 * own, 2 * LANES, 3 * LANES), BF16),
            vmem((2, blocks * padded, 3 * LANES), F32),
            vmem((own, padded, rows), F32),
            vmem((own, padded, rows), F32),
            vmem((2 * own, 4, 8, LANES), F32),
            vmem((padded, padded), BF16),
            vmem((padded, padded), BF16),
            vmem((padded, padded), F32),
            vmem(vert.shape, vert.dtype),
            vmem(loc.shape, loc.dtype),
            vmem(xidx.shape, xidx.dtype),
            pltpu.SMEM(alpha.shape, alpha.dtype),
            pltpu.SMEM(yidx.shape, yidx.dtype),
            dma((8,)),
            dma((6,)),
            dma((6,)),
            dma((SPAN,)),
            dma((SPAN,)),
            dma((SPAN,)),
            dma((SPAN,)),
            dma((groups,)),
            dma((groups,)),
            dma((mems, 4)),
            dma((mems, 4)),
        ],
        compiler_params=pltpu.CompilerParams(
            collective_id=0, has_side_effects=True, vmem_limit_bytes=40 * 2**20
        ),
    )(*operands)
    return jnp.swapaxes(result, 0, 1)[:slabs]


def solution(mesh):
    return jax.shard_map(
        functools.partial(body, mesh.shape["tile"], mesh.shape["mem"]),
        mesh=mesh,
        in_specs=(P(None, "tile", None), P(), P(), P(), P(), P(), P("mem", None, "tile", None)),
        out_specs=P(None, ("tile", "mem"), None),
        check_vma=False,
    )
```

```python
import functools

import jax
import jax.numpy as jnp
from jax import lax
from jax.experimental import pallas as pl
from jax.experimental.pallas import tpu as pltpu
from jax.sharding import PartitionSpec as P

MESH = pl.DeviceIdType.MESH
F32 = jnp.float32
BF16 = jnp.bfloat16
LANES = 128
SPAN = 16


def far_first(size):
    return sorted(range(1, size), key=lambda d: abs(2 * d - size))


def gains(a):
    return jnp.sqrt(1.0 - a * a), (1.0 - a * a) / jnp.sqrt(1.0 + a * a)


def extended(dst, matrix, pad, work):
    n = matrix.shape[-1]
    work[...] = jnp.zeros(work.shape, F32)
    work[0:n, 0:n] = matrix[0].astype(F32)
    i = lax.broadcasted_iota(jnp.int32, dst.shape, 0)
    j = lax.broadcasted_iota(jnp.int32, dst.shape, 1)
    keep = (i == j) & (i >= n) & (i < pad)
    dst[...] = jnp.where(keep, 1.0, work[...]).astype(BF16)


def kernel(
    tiles, mems, slabs,
    field, members, vert_hbm, loc_hbm, xidx_hbm, alpha_hbm, yidx_hbm,
    out,
    fbuf, mbuf, own_buf, x_own, x32, m32, far_s, far_r, side_s, side_r, hold, ax, gfx, gbx,
    send_z, recv_z, send_c, entering_all, send_y, recv_y, base, reach,
    lines, weights, mixed_all, smooth, acc, tab, lmat, vmat, square_work, vert, loc, xidx, alpha, yidx,
    local_sem, sm_s, sm_r, sz_s, sz_r, sc_s, sc_r, sy_s, sy_r, sx_s, sx_r,
):
    tile = lax.axis_index("tile")
    mem = lax.axis_index("mem")
    groups = tiles // SPAN
    q = lax.rem(tile, SPAN)
    y = tile // SPAN
    cols = field.shape[1]
    rows = field.shape[2]
    blocks = rows // LANES
    own = cols // mems
    levels = vert.shape[-1]
    padded = -(-slabs // 16) * 16
    pitch = x32.shape[1] // padded

    shift = (padded - slabs) * (mem // (mems - 1))
    get_own = pltpu.make_async_copy(
        field.at[pl.ds(16 * mem - shift, 16)], own_buf, local_sem.at[7]
    )
    get_own.start()

    barrier = pltpu.get_barrier_semaphore()

    for d in far_first(SPAN):
        pl.semaphore_signal(
            barrier,
            inc=1,
            device_id={"tile": y * SPAN + lax.rem(q + d, SPAN)},
            device_id_type=MESH,
        )

    for d in far_first(groups):
        pl.semaphore_signal(
            barrier,
            inc=1,
            device_id={"tile": lax.rem(y + d, groups) * SPAN + q},
            device_id_type=MESH,
        )

    for d in far_first(mems):
        pl.semaphore_signal(
            barrier, inc=1, device_id={"mem": lax.rem(mem + d, mems)}, device_id_type=MESH
        )

    small = [
        pltpu.make_async_copy(src, dst, local_sem.at[2 + at])
        for at, (src, dst) in enumerate(
            (
                (xidx_hbm, xidx),
                (alpha_hbm, alpha),
                (yidx_hbm, yidx),
                (loc_hbm, loc),
                (vert_hbm, vert),
            )
        )
    ]
    for copy in small:
        copy.start()
    get_field = pltpu.make_async_copy(field, fbuf, local_sem.at[1])
    get_field.start()
    get_members = pltpu.make_async_copy(members.at[0], mbuf, local_sem.at[0])
    get_members.start()

    for copy in small:
        copy.wait()
    sub = lax.broadcasted_iota(jnp.int32, (padded, LANES), 0)

    @pl.loop(0, blocks)
    def _(b):
        lane = pl.ds(pl.multiple_of(b * LANES, LANES), LANES)
        idx = xidx[:, lane]
        a = jnp.zeros(idx.shape, F32)
        for k in range(alpha.shape[0]):
            a = jnp.where(idx == k, alpha[k], a)
        wide = jnp.where(
            sub < levels,
            jnp.broadcast_to(a[0:1], (padded, LANES)),
            jnp.broadcast_to(a[1:2], (padded, LANES)),
        )
        fwd, back = gains(wide)
        ax[b] = wide
        gfx[b] = fwd
        gbx[b] = back

    def spread(src, dst, count, room):
        def put(view, s, i):
            for b in range(blocks):
                part = src[s, :, b * LANES : (b + 1) * LANES].astype(F32)
                view[b, i * pitch : i * pitch + cols, :] = part

        done = count // 8 * 8

        @pl.loop(0, count // 8)
        def _(g):
            at = pl.ds(pl.multiple_of(g * 8 * pitch, 8), 8 * pitch)
            view = dst.at[:, at, :]
            for i in range(8):
                put(view, 8 * g + i, i)

        for s in range(done, count):
            put(dst.at[:, done * pitch : room * pitch, :], s, s - done)
        for b in range(blocks):
            left = slice(count * pitch, room * pitch)
            dst[b, left, :] = jnp.zeros(((room - count) * pitch, LANES), F32)

    near = (lax.rem(mem + 1, mems), lax.rem(mem + mems - 1, mems))
    opposite = lax.rem(mem + 2, mems)
    halves = (slice(0, own // 2), slice(own // 2, own))

    def pass_far(side):
        return pltpu.make_async_remote_copy(
            src_ref=far_s.at[halves[side]],
            dst_ref=far_r.at[side],
            send_sem=sm_s.at[side],
            recv_sem=sm_r.at[side],
            device_id={"mem": near[side]},
            device_id_type=MESH,
        )

    def pass_near(side, half):
        return pltpu.make_async_remote_copy(
            src_ref=side_s.at[side, half],
            dst_ref=side_r.at[side, half],
            send_sem=sm_s.at[2 + 2 * side + half],
            recv_sem=sm_r.at[2 + 2 * side + half],
            device_id={"mem": near[side]},
            device_id_type=MESH,
        )

    wide_lanes = 2 * LANES
    half_own = own // 2

    def ensemble(peer, half, dst):
        @pl.loop(0, half_own)
        def _(k):
            col = peer * own + half * half_own + k

            def column(src):
                at = pl.ds(col, padded, stride=pitch)
                return jnp.concatenate([src[b, at, :] for b in range(blocks)], axis=1)

            m = column(m32)
            scaled = (m * column(x32)).astype(BF16)
            term = m * jnp.dot(lmat[...], scaled, preferred_element_type=F32)
            dst[k] = term.astype(dst.dtype)

    quads = padded // 16

    def local_states(b, p, src, first):
        at = pl.ds(pl.multiple_of(p * 16, 16), 16)
        a, fwd, back = ax[b, at, :], gfx[b, at, :], gbx[b, at, :]
        f = jnp.zeros((16, LANES), F32)
        states = []
        for c in range(cols):
            f = a * f + fwd * src[b, pl.ds(first * pitch + c, 16, stride=pitch), :]
            states.append(f)
        value = jnp.zeros((16, LANES), F32)
        backs = [None] * cols
        for c in reversed(range(cols)):
            value = a * value + back * states[c]
            backs[c] = value
        return states, backs

    def mine(values, k):
        value = values[k]
        for g in range(1, mems):
            value = jnp.where(mem == g, values[g * own + k], value)
        return value

    def to_span(src, dst, s_sem, r_sem, d):
        peer = lax.rem(q + d, SPAN)
        return pltpu.make_async_remote_copy(
            src_ref=src.at[peer],
            dst_ref=dst.at[q],
            send_sem=s_sem.at[peer],
            recv_sem=r_sem.at[q],
            device_id={"tile": y * SPAN + peer},
            device_id_type=MESH,
        )

    def from_span(src, dst, s_sem, r_sem, d):
        peer = lax.rem(q + d, SPAN)
        return pltpu.make_async_remote_copy(
            src_ref=src.at[peer],
            dst_ref=dst.at[peer],
            send_sem=s_sem.at[peer],
            recv_sem=r_sem.at[peer],
            device_id={"tile": y * SPAN + peer},
            device_id_type=MESH,
        )

    get_own.wait()
    spread(own_buf, x_own, 16, 16 + padded - slabs)

    @pl.loop(0, blocks)
    def _(b):
        states, backs = local_states(b, mem, x_own, shift)
        for h in range(2):
            part = slice(8 * h, 8 * h + 8)
            pair = jnp.concatenate([states[-1][part], backs[0][part]], axis=0)
            send_z[2 * b + h] = pair.astype(BF16)

    pl.semaphore_wait(barrier, (mems - 1) + (SPAN - 1) + (groups - 1))

    for d in far_first(SPAN):
        to_span(send_z, recv_z, sz_s, sz_r, d).start()

    recv_z[q] = send_z[q]

    extended(lmat, loc, slabs, square_work)
    extended(vmat, vert, slabs, square_work)
    get_field.wait()
    spread(fbuf, x32, slabs, padded)
    get_members.wait()
    spread(mbuf, m32, slabs, padded)
    for half in range(2):
        ensemble(opposite, half, far_s.at[halves[half]])
        pass_far(half).start()
    for side in range(2):
        ensemble(near[side], 1 - side, side_s.at[side, 1 - side])
        pass_near(side, 1 - side).start()

    zero = jnp.zeros((8, LANES), F32)
    piece_at = pl.ds(pl.multiple_of(mem * 16 + lax.rem(q, 2) * 8, 8), 8)
    a = ax[q // 2, piece_at, :]
    back = gbx[q // 2, piece_at, :]
    f = jnp.ones_like(a)
    states = []
    for c in range(cols):
        f = a * f
        states.append(f)
    cross = zero
    for c in reversed(range(cols)):
        cross = a * cross + back * states[c]
    decay = states[-1]
    square = decay * decay
    total, fade, far_decay = zero, jnp.ones_like(a), jnp.ones_like(a)
    for _ in range(SPAN):
        total = total + fade
        fade = fade * square
        far_decay = far_decay * decay
    far_cross = cross * total

    for d in far_first(SPAN):
        from_span(send_z, recv_z, sz_s, sz_r, d).wait_recv()

    def scan_span(f, b):
        enter_f, enter_b = [], [None] * SPAN
        pairs = [recv_z[i].astype(F32) for i in range(SPAN)]
        for i in range(SPAN):
            enter_f.append(f)
            f = pairs[i][0:8] + decay * f
        for i in reversed(range(SPAN)):
            enter_b[i] = b
            b = pairs[i][8:16] + cross * enter_f[i] + decay * b
        return f, b, enter_f, enter_b

    end, begin, _, _ = scan_span(zero, zero)
    send_y[...] = jnp.concatenate([end, begin], axis=0).astype(BF16)

    def to_group(d):
        peer = lax.rem(y + d, groups)
        return pltpu.make_async_remote_copy(
            src_ref=send_y,
            dst_ref=recv_y.at[y],
            send_sem=sy_s.at[peer],
            recv_sem=sy_r.at[y],
            device_id={"tile": peer * SPAN + q},
            device_id_type=MESH,
        )

    def from_group(d):
        peer = lax.rem(y + d, groups)
        return pltpu.make_async_remote_copy(
            src_ref=send_y,
            dst_ref=recv_y.at[peer],
            send_sem=sy_s.at[peer],
            recv_sem=sy_r.at[peer],
            device_id={"tile": peer * SPAN + q},
            device_id_type=MESH,
        )

    for d in far_first(groups):
        to_group(d).start()

    recv_y[y] = send_y[...]

    @pl.loop(0, blocks)
    def _(b):
        @pl.loop(0, quads)
        def _(p):
            _, backs = local_states(b, p, x32, p * 16)
            at = pl.ds(pl.multiple_of(b * padded + p * 16, 16), 16)
            for k in range(own):
                base[k, at, :] = mine(backs, k)

        for kind in range(2):
            at = slice(0, 16) if kind == 0 else slice(padded - 16, padded)
            a, back = ax[b, at, :], gbx[b, at, :]
            f = jnp.ones((16, LANES), F32)
            states = []
            for c in range(cols):
                f = a * f
                states.append(f)
            value = jnp.zeros((16, LANES), F32)
            backs = [None] * cols
            for c in reversed(range(cols)):
                value = a * value + back * states[c]
                backs[c] = value
            for k in range(own):
                reach[kind, b, 2 * k] = mine(backs, k)
                reach[kind, b, 2 * k + 1] = mine(states[::-1], k)

    for side in range(2):
        ensemble(near[side], side, hold.at[side])

    for d in far_first(groups):
        from_group(d).wait_recv()

    pairs = [recv_y[i].astype(F32) for i in range(groups)]
    enter = []
    f = zero
    mine_f = zero
    for i in range(groups):
        enter.append(f)
        mine_f = jnp.where(y == i, f, mine_f)
        f = pairs[i][0:8] + far_decay * f
    b = zero
    mine_b = zero
    for i in reversed(range(groups)):
        mine_b = jnp.where(y == i, b, mine_b)
        b = pairs[i][8:16] + far_cross * enter[i] + far_decay * b
    _, _, enter_f, enter_b = scan_span(mine_f, mine_b)
    for i in range(SPAN):
        send_c[i] = jnp.concatenate([enter_f[i], enter_b[i]], axis=0).astype(BF16)

    recv_c = entering_all.at[mem]

    for d in far_first(SPAN):
        to_span(send_c, recv_c, sc_s, sc_r, d).start()

    entering_all[mem, q] = send_c[q]

    for side in range(2):
        pass_far(side).wait_recv()

        @pl.loop(0, half_own)
        def _(k):
            total = hold[side, k] + far_r[side, k].astype(F32)
            side_s[side, side, k] = total.astype(BF16)

        pass_near(side, side).start()

    for half in range(2):
        ensemble(mem, half, acc.at[halves[half]])

    chunk = SPAN // 4

    def gather(d, c, source):
        at = entering_all.at[source, pl.ds(c * chunk, chunk)]
        return pltpu.make_async_remote_copy(
            src_ref=at,
            dst_ref=at,
            send_sem=sx_s.at[d, c],
            recv_sem=sx_r.at[d, c],
            device_id={"mem": lax.rem(mem + d, mems)},
            device_id_type=MESH,
        )

    for i in (0, 1, 3, 2):
        c = lax.rem(q // chunk + i, 4)
        for r in range(chunk):
            piece = c * chunk + r

            def returned(piece=piece):
                pltpu.make_async_remote_copy(
                    src_ref=send_c.at[piece],
                    dst_ref=recv_c.at[piece],
                    send_sem=sc_s.at[piece],
                    recv_sem=sc_r.at[piece],
                    device_id={"tile": y * SPAN + piece},
                    device_id_type=MESH,
                ).wait_recv()

            if i == 0:
                pl.when(piece != q)(returned)
            else:
                returned()
        for d in (2, 1, 3):
            gather(d, c, mem).start()

    lane8 = lax.broadcasted_iota(jnp.int32, (8, LANES), 1)
    sub8 = lax.broadcasted_iota(jnp.int32, (8, LANES), 0)
    row_i = lax.broadcasted_iota(jnp.int32, (LANES, LANES), 0)
    row_j = lax.broadcasted_iota(jnp.int32, (LANES, LANES), 1)

    def geometric(count, ratio):
        value = jnp.zeros(count.shape, F32)
        reached = jnp.ones(count.shape, F32)
        part = jnp.float32(1.0)
        for bit in range(8):
            has = (count & (1 << bit)) != 0
            value = jnp.where(has, value + reached * part, value)
            reached = jnp.where(has, reached * ratio, reached)
            part = part * (1.0 + ratio)
            ratio = ratio * ratio
        return value

    @pl.loop(0, own)
    def _(c):
        col = tile * cols + mem * own + c
        tables = []
        for kind in range(2):
            coeff = alpha[yidx[kind, col]]
            a = jnp.full((8, LANES), coeff, F32)
            fwd, back = gains(a)
            rate = jnp.log(jnp.maximum(a, 1e-37))

            def tall(x):
                return jnp.broadcast_to(x[0:1], (LANES, LANES))

            def power(exponent, log_a):
                return jnp.exp(exponent.astype(F32) * log_a)

            ratio = coeff * coeff
            inner = power(jnp.abs(row_i - row_j), tall(rate)) * tall(fwd * back)
            inner = inner * geometric(LANES - jnp.maximum(row_i, row_j), ratio)
            ends = power(LANES - 1 - row_i, tall(rate)) * tall(fwd)
            starts = jnp.broadcast_to(inner[:, 0:1], (LANES, LANES))
            for at, part in enumerate((inner, ends, starts)):
                high = part.astype(BF16)
                low = (part - high.astype(F32)).astype(BF16)
                lane = slice(at * LANES, (at + 1) * LANES)
                weights[2 * c + kind, 0:LANES, lane] = high
                weights[2 * c + kind, LANES : 2 * LANES, lane] = low
            far = coeff
            for _ in range(7):
                far = far * far
            whole = geometric(jnp.full((8, LANES), LANES, jnp.int32), ratio)
            tables.append(
                (
                    back * power(lane8 + 1, rate) * geometric(LANES - lane8, ratio),
                    power(LANES - lane8, rate),
                    jnp.full((8, LANES), far, F32),
                    back * a * whole,
                )
            )
        for at, (first, second) in enumerate(zip(*tables)):
            tab[2 * c, at] = first
            tab[2 * c + 1, at] = jnp.where(sub8 < levels % 8, first, second)

    def add_carries(p):
        kind = p // (quads - 1)
        for b in range(blocks):
            low = entering_all[p, 2 * b].astype(F32)
            high = entering_all[p, 2 * b + 1].astype(F32)
            f = jnp.concatenate([low[0:8], high[0:8]], axis=0)
            bk = jnp.concatenate([low[8:16], high[8:16]], axis=0)
            at = pl.ds(pl.multiple_of(b * padded + p * 16, 16), 16)
            for k in range(own):
                value = base[k, at, :] + reach[kind, b, 2 * k] * f + reach[kind, b, 2 * k + 1] * bk
                lines[k, at, :] = value.astype(BF16)

    add_carries(mem)
    for d in (1, 3, 2):
        source = lax.rem(mem + mems - d, mems)
        for c in range(4):
            gather(d, c, source).wait_recv()
        add_carries(source)

    for side in range(2):
        for half in range(2):
            pass_near(side, half).wait_recv()

    last = padded - 8

    for c in range(own):
        x = jnp.concatenate([lines[c], lines[c]], axis=1)
        mixed = mixed_all.at[c % 2]
        mixed[...] = jnp.dot(x, weights[2 * c], preferred_element_type=F32)
        tail = jnp.concatenate(
            [lines[c, (b + 1) * padded - 16 : (b + 1) * padded, :] for b in range(blocks)], axis=0
        )
        tail = jnp.concatenate([tail, tail], axis=1)
        other = jnp.dot(tail, weights[2 * c + 1], preferred_element_type=F32)
        pick = jnp.concatenate([sub8] * 3, axis=1) < levels % 8
        for b in range(blocks):
            at = slice(b * padded + last, (b + 1) * padded)
            mixed[at, :] = jnp.where(pick, mixed[at, :], other[16 * b + 8 : 16 * b + 16])

        for g in range(padded // 8):
            t = 2 * c + g // (levels // 8)
            from_left, from_right, far, cross = tab[t, 0], tab[t, 1], tab[t, 2], tab[t, 3]

            def block(b, part):
                at = slice(b * padded + g * 8, b * padded + g * 8 + 8)
                return mixed[at, part * LANES : (part + 1) * LANES]

            state = jnp.zeros((8, LANES), F32)
            entering = []
            for b in range(blocks):
                entering.append(state)
                state = block(b, 1) + far * state
            state = jnp.zeros((8, LANES), F32)
            for b in reversed(range(blocks)):
                value = block(b, 0) + from_left * entering[b] + from_right * state
                smooth[c, g * 8 : g * 8 + 8, b * LANES : (b + 1) * LANES] = value
                state = block(b, 2) + cross * entering[b] + far * state

        for w in range(rows // wide_lanes):
            lane = slice(w * wide_lanes, (w + 1) * wide_lanes)
            others = side_r[0, c // half_own, c % half_own, :, lane].astype(F32)
            others = others + side_r[1, c // half_own, c % half_own, :, lane].astype(F32)
            x = smooth[c, :, lane].astype(BF16)
            static = jnp.dot(vmat[...], x, preferred_element_type=F32)
            out[c, :, lane] = (static + (acc[c, :, lane] + others) / (mems - 1)).astype(BF16)

    for d in (1, 2, 3):
        for c in range(4):
            gather(d, c, mem).wait_send()
    for side in range(2):
        pass_far(side).wait_send()
        for half in range(2):
            pass_near(side, half).wait_send()

    for d in far_first(SPAN):
        to_span(send_z, recv_z, sz_s, sz_r, d).wait_send()
        to_span(send_c, recv_c, sc_s, sc_r, d).wait_send()

    for d in far_first(groups):
        to_group(d).wait_send()


def body(tiles, mems, field, vert, loc, alpha, xidx, yidx, members):
    slabs, cols, rows = field.shape
    own = cols // mems
    padded = -(-slabs // 16) * 16
    blocks = rows // LANES
    groups = tiles // SPAN
    dma = pltpu.SemaphoreType.DMA
    vmem = pltpu.VMEM
    operands = [
        pltpu.with_memory_space_constraint(x, pltpu.HBM)
        for x in (field, members, vert, loc, xidx, alpha, yidx)
    ]
    result = pl.pallas_call(
        functools.partial(kernel, tiles, mems, slabs),
        out_shape=jax.ShapeDtypeStruct((own, padded, rows), BF16),
        in_specs=[pl.BlockSpec(memory_space=pl.ANY)] * 7,
        out_specs=pl.BlockSpec(memory_space=pltpu.VMEM),
        scratch_shapes=[
            vmem((slabs, cols, rows), BF16),
            vmem((slabs, cols, rows), BF16),
            vmem((16, cols, rows), BF16),
            vmem((blocks, -(-(16 + padded - slabs) * (cols + 1) // 8) * 8, LANES), F32),
            vmem((blocks, padded * (cols + 1), LANES), F32),
            vmem((blocks, padded * (cols + 1), LANES), F32),
            vmem((own, padded, rows), BF16),
            vmem((2, own // 2, padded, rows), BF16),
            vmem((2, 2, own // 2, padded, rows), BF16),
            vmem((2, 2, own // 2, padded, rows), BF16),
            vmem((2, own // 2, padded, rows), F32),
            vmem((blocks, padded, LANES), F32),
            vmem((blocks, padded, LANES), F32),
            vmem((blocks, padded, LANES), F32),
            vmem((SPAN, 16, LANES), BF16),
            vmem((SPAN, 16, LANES), BF16),
            vmem((SPAN, 16, LANES), BF16),
            vmem((mems, SPAN, 16, LANES), BF16),
            vmem((16, LANES), BF16),
            vmem((groups, 16, LANES), BF16),
            vmem((own, blocks * padded, LANES), F32),
            vmem((2, blocks, 2 * own, 16, LANES), F32),
            vmem((own, blocks * padded, LANES), BF16),
            vmem((2 * own, 2 * LANES, 3 * LANES), BF16),
            vmem((2, blocks * padded, 3 * LANES), F32),
            vmem((own, padded, rows), F32),
            vmem((own, padded, rows), F32),
            vmem((2 * own, 4, 8, LANES), F32),
            vmem((padded, padded), BF16),
            vmem((padded, padded), BF16),
            vmem((padded, padded), F32),
            vmem(vert.shape, vert.dtype),
            vmem(loc.shape, loc.dtype),
            vmem(xidx.shape, xidx.dtype),
            pltpu.SMEM(alpha.shape, alpha.dtype),
            pltpu.SMEM(yidx.shape, yidx.dtype),
            dma((8,)),
            dma((6,)),
            dma((6,)),
            dma((SPAN,)),
            dma((SPAN,)),
            dma((SPAN,)),
            dma((SPAN,)),
            dma((groups,)),
            dma((groups,)),
            dma((mems, 4)),
            dma((mems, 4)),
        ],
        compiler_params=pltpu.CompilerParams(
            collective_id=0, has_side_effects=True, vmem_limit_bytes=40 * 2**20
        ),
    )(*operands)
    return jnp.swapaxes(result, 0, 1)[:slabs]


def solution(mesh):
    return jax.shard_map(
        functools.partial(body, mesh.shape["tile"], mesh.shape["mem"]),
        mesh=mesh,
        in_specs=(P(None, "tile", None), P(), P(), P(), P(), P(), P("mem", None, "tile", None)),
        out_specs=P(None, ("tile", "mem"), None),
        check_vma=False,
    )
```
